768 devices in a mesh: ctx: 96 (over x, z, core), tp: 8 (over y).
Axes of the slice: x: 4, y: 8, z: 12, core: 2. Of those that a mesh axis runs over, the one named last changes fastest.
Arguments:
- query: bfloat16 [12288, 8192], P('ctx', 'tp'), may hold values from -6 to 6
- keys: bfloat16 [12288, 8192], P('ctx', 'tp'), may hold values from -6 to 6
- values: bfloat16 [12288, 8192], P('ctx', 'tp'), may hold values from -6 to 6
- rates: float32 [16, 8192], P(None, 'tp'), may hold values from 4.0690105e-05 to 0.03
- residues: float32 [16, 8192], P(None, 'tp'), may hold values from -3 to 3
- skip: float32 [8192], P('tp'), may hold values from 0.25 to 1.5
- gain: float32 [8192], P('tp'), may hold values from 0.25 to 1.75
Outputs:
- mixed: bfloat16 [12288, 8192], P('ctx', 'tp')
The draws below stay inside these ranges and needn't reach their ends.
All inputs are finite; a program needn't handle non-finite values.
Results may differ from the reference program's by a relative error of at most 0.0025.
Values sent between devices are 32-bit elements; how exact they have to be, the bound alone decides.
A program may use at most 32 MiB of HBM per device.

```python
import math
import jax
import jax.numpy as jnp
from jax import lax

C = 8192
M = 16
TOKENS = 12288


def block_levels(key, shape, shards, least, largest):
    def one(position, shards_of):
        steps = jax.random.uniform(jax.random.fold_in(jax.random.fold_in(key, 6), position), (shards_of,), jnp.float32, least / len(shards), largest / len(shards))
        return jnp.repeat(jnp.exp(steps), shape[position] // shards_of).reshape((-1,) + (1,) * (len(shape) - position - 1))

    loudness = one(*shards[0])
    for cut in shards[1:]:
        loudness = loudness * one(*cut)
    return loudness


def noise(rng, shape, scale, most, cuts=(), kind=jnp.bfloat16):
    drawn = jax.random.normal(rng, shape, jnp.float32) * scale
    if len(cuts) > 0:
        drawn = block_levels(rng, shape, cuts, -0.22, 0.18) * drawn
    return jnp.clip(drawn, min=-most, max=most).astype(kind)


def setup_inputs(seed: int = 0) -> dict:
    streams_of = jax.random.split(jax.random.key(seed), 8)
    return {
        "query": noise(streams_of[0], (TOKENS, C), 1.0, 6.0, ((0, 96), (1, 8))),
        "keys": noise(streams_of[1], (TOKENS, C), 1.0, 6.0, ((0, 96), (1, 8))),
        "values": noise(streams_of[2], (TOKENS, C), 1.0, 6.0, ((0, 96), (1, 8))),
        "rates": jnp.clip(jnp.exp(math.log(0.03) - 6.6029677 * jax.random.uniform(streams_of[3], (M, C), jnp.float32) ** block_levels(streams_of[3], (M, C), ((1, 8),), -0.2, 0.2)), 4.069010537932627e-05, 0.03),
        "residues": noise(streams_of[4], (M, C), 0.5, 3.0, ((1, 8),), jnp.float32),
        "skip": jnp.clip(0.25 + 1.25 * jax.random.uniform(streams_of[5], (C,), jnp.float32) ** block_levels(streams_of[5], (C,), ((0, 8),), -0.2, 0.2), 0.25, 1.5),
        "gain": jnp.clip(1.0 + 0.15 * jax.random.normal(streams_of[6], (C,), jnp.float32), 0.25, 1.75),
    }


def combine_pair(first, second):
    return (first[0] * second[0], first[1] * second[0] + second[1])

def channel_block(items):
    driven, rates, residues = items

    def one_mode(total, mode):
        rate, residue = mode
        decay = jnp.exp(-rate)
        scale = residue * jnp.sqrt(1.0 - decay * decay)
        factors = jnp.broadcast_to(decay[None, :], driven.shape)
        state = lax.associative_scan(combine_pair, (factors, driven), axis=0)[1]
        return (total + scale[None, :] * state, None)
    start = jnp.zeros(driven.shape, jnp.float32)
    total, unused = lax.scan(one_mode, start, (rates, residues))
    return total

def reference(query, keys, values, rates, residues, skip, gain):
    driven = keys.astype(jnp.float32) * values.astype(jnp.float32)
    width = min(C, 1024)
    blocks = C // width
    driven_blocks = driven.reshape(TOKENS, blocks, width).transpose(1, 0, 2)
    rate_blocks = rates.reshape(M, blocks, width).transpose(1, 0, 2)
    residue_blocks = residues.reshape(M, blocks, width).transpose(1, 0, 2)
    filtered = lax.map(channel_block, (driven_blocks, rate_blocks, residue_blocks))
    filtered = filtered.transpose(1, 0, 2).reshape(TOKENS, C)
    gated = query.astype(jnp.float32) * (filtered + skip[None, :] * driven)
    power = lax.optimization_barrier(jnp.mean(gated * gated, axis=1))
    return (gated * lax.rsqrt(power + 1e-06)[:, None] * gain[None, :]).astype(jnp.bfloat16)
```

```python
import functools

import jax
import jax.numpy as jnp
from jax import lax
from jax.experimental import pallas as pl
from jax.experimental.pallas import tpu as pltpu
from jax.sharding import PartitionSpec as P

MESH = pl.DeviceIdType.MESH
F32 = jnp.float32

C = 8192
NX, NZ, NY = 4, 12, 8
LANES = 128
M = 16
COUNT = 128
WIDTH = 1024
LB = WIDTH // LANES
GROUP = 4
GROUPS = NZ // GROUP
MEMBERS = 2 * GROUP
PIECES = 4
PM = M // PIECES
BLOCKS = COUNT // 8


def token_row(block, s):
    return pl.ds(block * 64 + s, 8, stride=8)


def kernel(q_hbm, k_hbm, v_hbm, rates_hbm, res_hbm, skip_hbm, gain_hbm, o_ref,
           q_ref, k_ref, v_ref, rates_ref, res_ref, skip_ref, gain_ref,
           driven, relay, dec, scale, ends, fwd_buf, total, ex_buf, row_total, x_buf,
           start_state, back_src, carry, conv, base, squares, part, parts, inv,
           in_sem, fwd_send, fwd_recv, ex_send, ex_recv, x_send, x_recv,
           back_send, back_recv, y_send, y_recv):
    ctx = lax.axis_index("ctx")
    y = lax.axis_index("tp")
    core = lax.rem(ctx, 2)
    chip = lax.div(ctx, 2)
    z = lax.rem(chip, NZ)
    x = lax.div(chip, NZ)
    g = lax.div(z, GROUP)
    r = lax.rem(z, GROUP)
    me = r * 2 + core
    is_owner = jnp.logical_and(r >= 1, r <= 2)
    my_piece = jnp.where(is_owner, (r - 1) * 2 + core, 0)

    def device(dx, dz, dc, dy):
        return ((dx * NZ + dz) * 2 + dc, dy)

    def owner_device(p):
        return device(x, g * GROUP + 1 + p // 2, p % 2, y)

    def member_device(j):
        return device(x, g * GROUP + j // 2, j % 2, y)

    loads = []
    for n, (src, dst) in enumerate((
            (k_hbm, k_ref), (v_hbm, v_ref), (rates_hbm, rates_ref), (res_hbm, res_ref),
            (q_hbm, q_ref), (skip_hbm, skip_ref), (gain_hbm, gain_ref))):
        load = pltpu.make_async_copy(src, dst, in_sem.at[n])
        load.start()
        loads.append(load)

    barrier = pltpu.get_barrier_semaphore()

    def greet(dev):
        pl.semaphore_signal(barrier, inc=1, device_id=dev, device_id_type=MESH)

    for p in range(PIECES):
        @pl.when(jnp.logical_not(jnp.logical_and(is_owner, my_piece == p)))
        def _(p=p):
            greet(owner_device(p))
    for k in range(1, NY):
        greet(device(x, z, core, lax.rem(y + k, NY)))

    @pl.when(is_owner)
    def _():
        for j in (0, 1, 6, 7):
            greet(member_device(j))
        for k in range(1, GROUPS):
            greet(device(x, lax.rem(z + GROUP * k, NZ), core, y))
        for k in range(1, NX):
            greet(device(lax.rem(x + k, NX), z, core, y))

    loads[2].wait()
    loads[3].wait()
    for which, (src, dst) in enumerate(((rates_ref, dec), (res_ref, scale))):
        for b in range(M // 8):
            for j in range(LB):
                relay[which * 128 + (b * 8 + j) * 8:which * 128 + (b * 8 + j) * 8 + 8, :] = (
                    src[b * 8:b * 8 + 8, j * LANES:(j + 1) * LANES])

    def mode_rate(m):
        return relay[token_row(m // 8, m % 8), :]

    for m in range(M):
        d = jnp.exp(-mode_rate(m))
        dec[m] = d
        scale[m] = relay[pl.ds(128 + (m // 8) * 64 + m % 8, 8, stride=8), :] * jnp.sqrt(1.0 - d * d)

    loads[0].wait()
    loads[1].wait()

    def make_driven(b, _):
        rows = pl.ds(pl.multiple_of(b * 16, 16), 16)
        for j in range(LB):
            cols = slice(j * LANES, (j + 1) * LANES)
            d = k_ref[rows, cols].astype(F32) * v_ref[rows, cols].astype(F32)
            driven[pl.ds(pl.multiple_of(b * 128 + j * 8, 8), 8), :] = d[:8]
            driven[pl.ds(pl.multiple_of(b * 128 + 64 + j * 8, 8), 8), :] = d[8:]
        return 0

    lax.fori_loop(0, COUNT // 16, make_driven, 0)

    def fwd_copy(p):
        return pltpu.make_async_remote_copy(
            src_ref=ends.at[pl.ds(p * PM, PM)], dst_ref=fwd_buf.at[me],
            send_sem=fwd_send.at[p], recv_sem=fwd_recv.at[me],
            device_id=owner_device(p), device_id_type=MESH)

    SEGS = 4
    SEG_BLOCKS = BLOCKS // SEGS

    for p in range(PIECES):
        decays = [dec[p * PM + i] for i in range(PM)]

        def steps(b, states, decays=decays):
            states = list(states)
            for s in range(8):
                for seg in range(SEGS):
                    d = driven[token_row(seg * SEG_BLOCKS + b, s), :]
                    for i in range(PM):
                        n = seg * PM + i
                        states[n] = states[n] * decays[i] + d
            return tuple(states)

        zero = jnp.zeros((8, LANES), F32)
        states = lax.fori_loop(0, SEG_BLOCKS, steps, (zero,) * (SEGS * PM))
        for i in range(PM):
            m = p * PM + i
            leap = jnp.exp(-mode_rate(m) * (COUNT // SEGS))
            s = states[i]
            for seg in range(1, SEGS):
                s = s * leap + states[seg * PM + i]
            ends[m] = s
        if p == 0:
            pl.semaphore_wait(barrier, jnp.where(is_owner, 7 + 7 + GROUPS - 1 + NX - 1, PIECES + 7))

        @pl.when(jnp.logical_not(jnp.logical_and(is_owner, my_piece == p)))
        def _(p=p):
            fwd_copy(p).start()

    def conv_steps(b, states):
        states = list(states)
        for s in range(8):
            d = driven[token_row(b, s), :]
            terms = []
            for m in range(M):
                states[m] = states[m] * dec[m] + d
                terms.append(states[m] * scale[m])
            while len(terms) > 1:
                terms = [terms[i] + terms[i + 1] for i in range(0, len(terms), 2)]
            conv[pl.ds(pl.multiple_of(b * 64 + s * 8, 8), 8), :] = terms[0]
        return tuple(states)

    zero = jnp.zeros((8, LANES), F32)
    lax.fori_loop(0, BLOCKS, conv_steps, (zero,) * M)

    loads[4].wait()
    loads[5].wait()
    loads[6].wait()

    def make_base(b, _):
        rows = pl.ds(pl.multiple_of(b * 16, 16), 16)
        for j in range(LB):
            q = q_ref[rows, j * LANES:(j + 1) * LANES].astype(F32)
            gate = skip_ref[j:j + 1, :]
            for h in range(2):
                at = pl.ds(pl.multiple_of(b * 128 + h * 64 + j * 8, 8), 8)
                local = conv[pl.ds(b * 128 + h * 64 + j, 8, stride=8), :]
                base[at, :] = q[h * 8:h * 8 + 8] * (local + gate * driven[at, :])
        return 0

    lax.fori_loop(0, COUNT // 16, make_base, 0)

    def back_copy(j):
        return pltpu.make_async_remote_copy(
            src_ref=back_src.at[j], dst_ref=carry.at[my_piece],
            send_sem=back_send.at[j], recv_sem=back_recv.at[my_piece],
            device_id=member_device(j), device_id_type=MESH)

    def ex_copy(k):
        return pltpu.make_async_remote_copy(
            src_ref=total, dst_ref=ex_buf.at[k - 1],
            send_sem=ex_send.at[k - 1], recv_sem=ex_recv.at[k - 1],
            device_id=device(x, lax.rem(z + GROUP * k, NZ), core, y), device_id_type=MESH)

    def x_copy(k):
        return pltpu.make_async_remote_copy(
            src_ref=row_total, dst_ref=x_buf.at[x],
            send_sem=x_send.at[k - 1], recv_sem=x_recv.at[x],
            device_id=device(lax.rem(x + k, NX), z, core, y), device_id_type=MESH)

    @pl.when(is_owner)
    def _():
        def rate_of(i):
            m = my_piece * PM + i
            return relay[pl.ds(lax.div(m, 8) * 64 + lax.rem(m, 8), 8, stride=8), :]

        mine = [rate_of(i) for i in range(PM)]
        hop = [jnp.exp(-rt * COUNT) for rt in mine]
        for j in range(MEMBERS):
            @pl.when(me != j)
            def _(j=j):
                pltpu.make_async_remote_copy(
                    src_ref=ends.at[pl.ds(0, PM)], dst_ref=fwd_buf.at[j],
                    send_sem=fwd_send.at[0], recv_sem=fwd_recv.at[j],
                    device_id=member_device(j), device_id_type=MESH).wait_recv()

        @pl.loop(0, PM)
        def _(i):
            fwd_buf[me, i] = ends[my_piece * PM + i]

        for i in range(PM):
            s = fwd_buf[0, i]
            for j in range(1, MEMBERS):
                s = s * hop[i] + fwd_buf[j, i]
            total[i] = s
        for k in range(1, GROUPS):
            ex_copy(k).start()
        for k in range(1, GROUPS):
            ex_copy(k).wait_recv()

        span = float(COUNT * MEMBERS)
        gf = g.astype(F32)
        for i in range(PM):
            rate = mine[i]
            row = total[i] * jnp.exp(-rate * (span * (GROUPS - 1 - gf)))
            before = zero
            for k in range(1, GROUPS):
                src = lax.rem(g - k + GROUPS, GROUPS)
                sf = src.astype(F32)
                row = row + ex_buf[k - 1, i] * jnp.exp(-rate * (span * (GROUPS - 1 - sf)))
                gap = jnp.maximum(gf - 1.0 - sf, 0.0)
                before = before + jnp.where(src < g, 1.0, 0.0) * (ex_buf[k - 1, i] * jnp.exp(-rate * (span * gap)))
            row_total[i] = row
            start_state[i] = before
        for k in range(1, NX):
            @pl.when(x + k < NX)
            def _(k=k):
                x_copy(k).start()
        row_span = span * GROUPS
        for src in range(NX - 1):
            @pl.when(src < x)
            def _(src=src):
                pltpu.make_async_remote_copy(
                    src_ref=row_total, dst_ref=x_buf.at[src],
                    send_sem=x_send.at[0], recv_sem=x_recv.at[src],
                    device_id=device(src, z, core, y), device_id_type=MESH).wait_recv()
                tokens = (x - 1 - src).astype(F32) * row_span + gf * span
                for i in range(PM):
                    start_state[i] = start_state[i] + x_buf[src, i] * jnp.exp(-mine[i] * tokens)
        for j in range(MEMBERS):
            for i in range(PM):
                if j == 0:
                    back_src[0, i] = start_state[i]
                else:
                    back_src[j, i] = back_src[j - 1, i] * hop[i] + fwd_buf[j - 1, i]

            @pl.when(me != j)
            def _(j=j):
                back_copy(j).start()

            @pl.when(me == j)
            def _(j=j):
                for i in range(PM):
                    carry[my_piece, i] = back_src[j, i]

    for p in range(PIECES):
        @pl.when(jnp.logical_not(jnp.logical_and(is_owner, my_piece == p)))
        def _(p=p):
            pltpu.make_async_remote_copy(
                src_ref=back_src.at[0], dst_ref=carry.at[p],
                send_sem=back_send.at[0], recv_sem=back_recv.at[p],
                device_id=owner_device(p), device_id_type=MESH).wait_recv()

    def carry_steps(b, states):
        states = list(states)
        for s in range(8):
            for m in range(M):
                states[m] = states[m] * dec[m]
            terms = states
            while len(terms) > 1:
                terms = [terms[i] + terms[i + 1] for i in range(0, len(terms), 2)]
            conv[pl.ds(pl.multiple_of(b * 64 + s * 8, 8), 8), :] = terms[0]
        return tuple(states)

    lax.fori_loop(0, BLOCKS, carry_steps,
                  tuple(carry[m // PM, m % PM] * scale[m] for m in range(M)))

    def gate_block(b, _):
        rows = pl.ds(pl.multiple_of(b * 16, 16), 16)
        sums = [jnp.zeros((8, LANES), F32)] * 2
        for j in range(LB):
            q = q_ref[rows, j * LANES:(j + 1) * LANES].astype(F32)
            for h in range(2):
                at = pl.ds(pl.multiple_of(b * 128 + h * 64 + j * 8, 8), 8)
                far = conv[pl.ds(b * 128 + h * 64 + j, 8, stride=8), :]
                gated = base[at, :] + q[h * 8:h * 8 + 8] * far
                base[at, :] = gated
                sums[h] = sums[h] + gated * gated
        squares[pl.ds(pl.multiple_of(b * 16, 8), 8), :] = sums[0]
        squares[pl.ds(pl.multiple_of(b * 16 + 8, 8), 8), :] = sums[1]
        return 0

    lax.fori_loop(0, COUNT // 16, gate_block, 0)

    weight = jnp.full((8, LANES), 1.0 / (8 * C), F32)
    part[...] = lax.dot_general(
        weight, squares[...], (((1,), (1,)), ((), ())),
        precision=lax.Precision.HIGHEST, preferred_element_type=F32)

    def y_copy(k):
        return pltpu.make_async_remote_copy(
            src_ref=part, dst_ref=parts.at[y],
            send_sem=y_send.at[k - 1], recv_sem=y_recv.at[y],
            device_id=device(x, z, core, lax.rem(y + k, NY)), device_id_type=MESH)

    for k in range(1, NY):
        y_copy(k).start()
    parts[y] = part[...]
    for k in range(1, NY):
        src = lax.rem(y + k, NY)
        pltpu.make_async_remote_copy(
            src_ref=part, dst_ref=parts.at[src],
            send_sem=y_send.at[0], recv_sem=y_recv.at[src],
            device_id=device(x, z, core, src), device_id_type=MESH).wait_recv()
    power = lax.dot_general(
        parts[...].reshape(NY * 8, LANES), jnp.ones((NY * 8, LANES), F32), (((0,), (0,)), ((), ())),
        precision=lax.Precision.HIGHEST, preferred_element_type=F32)
    inv[...] = lax.rsqrt(power + 1e-06)

    def finish(b, _):
        rows = pl.ds(pl.multiple_of(b * 16, 16), 16)
        for j in range(LB):
            level = gain_ref[j:j + 1, :]
            halves = []
            for h in range(2):
                at = pl.ds(pl.multiple_of(b * 128 + h * 64 + j * 8, 8), 8)
                norm = inv[pl.ds(pl.multiple_of(b * 16 + h * 8, 8), 8), :]
                halves.append(base[at, :] * norm * level)
            o_ref[rows, j * LANES:(j + 1) * LANES] = jnp.concatenate(halves, axis=0).astype(jnp.bfloat16)
        return 0

    lax.fori_loop(0, COUNT // 16, finish, 0)

    for p in range(PIECES):
        @pl.when(jnp.logical_not(jnp.logical_and(is_owner, my_piece == p)))
        def _(p=p):
            fwd_copy(p).wait_send()

    @pl.when(is_owner)
    def _():
        for k in range(1, GROUPS):
            ex_copy(k).wait_send()
        for k in range(1, NX):
            @pl.when(x + k < NX)
            def _(k=k):
                x_copy(k).wait_send()
        for j in range(MEMBERS):
            @pl.when(me != j)
            def _(j=j):
                back_copy(j).wait_send()
    for k in range(1, NY):
        y_copy(k).wait_send()


def body(query, keys, values, rates, residues, skip, gain):
    any_space = pl.BlockSpec(memory_space=pl.ANY)
    vmem = pltpu.VMEM
    dma = pltpu.SemaphoreType.DMA
    tile = (8, LANES)
    return pl.pallas_call(
        kernel,
        name="modal_scan",
        out_shape=jax.ShapeDtypeStruct((COUNT, WIDTH), jnp.bfloat16),
        in_specs=[any_space] * 7,
        out_specs=pl.BlockSpec(memory_space=pltpu.VMEM),
        scratch_shapes=[
            vmem((COUNT, WIDTH), jnp.bfloat16),
            vmem((COUNT, WIDTH), jnp.bfloat16),
            vmem((COUNT, WIDTH), jnp.bfloat16),
            vmem((M, WIDTH), F32),
            vmem((M, WIDTH), F32),
            vmem(tile, F32),
            vmem(tile, F32),
            vmem((COUNT * 8, LANES), F32),
            vmem((256, LANES), F32),
            vmem((M,) + tile, F32),
            vmem((M,) + tile, F32),
            vmem((M,) + tile, F32),
            vmem((MEMBERS, PM) + tile, F32),
            vmem((PM,) + tile, F32),
            vmem((GROUPS - 1, PM) + tile, F32),
            vmem((PM,) + tile, F32),
            vmem((NX, PM) + tile, F32),
            vmem((PM,) + tile, F32),
            vmem((MEMBERS, PM) + tile, F32),
            vmem((PIECES, PM) + tile, F32),
            vmem((COUNT * 8, LANES), F32),
            vmem((COUNT * 8, LANES), F32),
            vmem((COUNT, LANES), F32),
            vmem(tile, F32),
            vmem((NY,) + tile, F32),
            vmem((COUNT, LANES), F32),
            dma((7,)),
            dma((PIECES,)), dma((MEMBERS,)),
            dma((GROUPS - 1,)), dma((GROUPS - 1,)),
            dma((NX - 1,)), dma((NX,)),
            dma((MEMBERS,)), dma((PIECES,)),
            dma((NY - 1,)), dma((NY,)),
        ],
        compiler_params=pltpu.CompilerParams(collective_id=0, has_side_effects=True),
    )(query, keys, values, rates, residues, skip.reshape(LB, LANES), gain.reshape(LB, LANES))


def solution(mesh):
    in_specs = (
        P("ctx", "tp"), P("ctx", "tp"), P("ctx", "tp"),
        P(None, "tp"), P(None, "tp"), P("tp"), P("tp"),
    )
    return jax.shard_map(body, mesh=mesh, in_specs=in_specs, out_specs=P("ctx", "tp"), check_vma=False)
```

```python
import jax
import jax.numpy as jnp
from jax import lax
from jax.experimental import pallas as pl
from jax.experimental.pallas import tpu as pltpu
from jax.sharding import PartitionSpec as P

MESH = pl.DeviceIdType.MESH
F32 = jnp.float32

C = 8192
NX, NZ, NY = 4, 12, 8
LANES = 128
M = 16
COUNT = 128
WIDTH = 1024
LB = WIDTH // LANES
GROUP = 4
GROUPS = NZ // GROUP
MEMBERS = 2 * GROUP
PIECES = 4
PM = M // PIECES
BLOCKS = COUNT // 8
SEGS = 4
OWNER_BASE = (0, 0, 1)
NEAR = 4
SEG_BLOCKS = BLOCKS // SEGS


def token_row(block, s):
    return pl.ds(block * 64 + s, 8, stride=8)


def kernel(q_hbm, k_hbm, v_hbm, rates_hbm, res_hbm, skip_hbm, g_ref, inv_ref,
           q_ref, k_ref, v_ref, rates_ref, res_ref, skip_ref,
           driven, relay, dec, scale, leap, ends, fwd_buf, total, x_buf, rows_before, rows_with,
           ex_buf, far_buf, far_coef, coef,
           start_state, back_src, carry, conv, base, squares, part, parts,
           in_sem, fwd_send, fwd_recv, x_send, x_recv, ex_send, ex_recv, far_send, far_recv,
           back_send, back_recv, y_send, y_recv, x_ready, ex_ready, y_ready):
    ctx = lax.axis_index("ctx")
    y = lax.axis_index("tp")
    core = lax.rem(ctx, 2)
    chip = lax.div(ctx, 2)
    z = lax.rem(chip, NZ)
    x = lax.div(chip, NZ)
    g = lax.div(z, GROUP)
    r = lax.rem(z, GROUP)
    me = r * 2 + core
    first = g == 0
    owner_base = jnp.where(g == 2, OWNER_BASE[2], OWNER_BASE[0])
    is_owner = jnp.logical_and(r >= owner_base, r <= owner_base + 1)
    pair = jnp.where(r <= owner_base, 0, 1)
    y_rank = jnp.where(y < NY // 2, y, NY + NY // 2 - 1 - y)
    my_piece = pair * 2 + core
    has_rows = x >= 1

    def device(dx, dz, dc, dy):
        return ((dx * NZ + dz) * 2 + dc, dy)

    def owner_device(p):
        return device(x, g * GROUP + owner_base + lax.div(p, 2), lax.rem(p, 2), y)

    def peer_owner(group):
        return device(x, group * GROUP + OWNER_BASE[group] + pair, core, y)

    def is_me(p):
        return jnp.logical_and(is_owner, my_piece == p)

    def member_device(j):
        return device(x, g * GROUP + j // 2, j % 2, y)

    loads = []
    for n, (src, dst) in enumerate((
            (k_hbm, k_ref), (v_hbm, v_ref), (rates_hbm, rates_ref), (res_hbm, res_ref),
            (q_hbm, q_ref), (skip_hbm, skip_ref))):
        load = pltpu.make_async_copy(src, dst, in_sem.at[n])
        load.start()
        loads.append(load)

    barrier = pltpu.get_barrier_semaphore()

    def greet(dev):
        pl.semaphore_signal(barrier, inc=1, device_id=dev, device_id_type=MESH)

    def ready(sem, dev):
        pl.semaphore_signal(sem, inc=1, device_id=dev, device_id_type=MESH)

    def earlier_y(act):
        for k in range(1, NY):
            other = lax.rem(y + k, NY)
            rank = jnp.where(other < NY // 2, other, NY + NY // 2 - 1 - other)

            @pl.when(rank < y_rank)
            def _(other=other):
                act(device(x, z, core, other))

    for p in range(PIECES):
        @pl.when(jnp.logical_not(is_me(p)))
        def _(p=p):
            greet(owner_device(jnp.int32(p)))
    for k in range(1, NY):
        other = lax.rem(y + k, NY)
        rank = jnp.where(other < NY // 2, other, NY + NY // 2 - 1 - other)

        @pl.when(rank > y_rank)
        def _(other=other):
            greet(device(x, z, core, other))

    takes_far = jnp.logical_and(jnp.logical_and(first, r < NEAR // 2), has_rows)

    @pl.when(takes_far)
    def _():
        for group in range(1, GROUPS):
            for p in range(PIECES):
                greet(device(x, group * GROUP + OWNER_BASE[group] + p // 2, p % 2, y))

    @pl.when(is_owner)
    def _():
        for j in range(MEMBERS):
            @pl.when(jnp.logical_or(j // 2 < owner_base, j // 2 > owner_base + 1))
            def _(j=j):
                greet(member_device(j))
        for k in range(1, NX):
            @pl.when(x + k < NX)
            def _(k=k):
                greet(device(lax.rem(x + k, NX), z, core, y))

        @pl.when(first)
        def _():
            greet(peer_owner(1))

        @pl.when(g <= 1)
        def _():
            greet(peer_owner(2))

    expected = y_rank + jnp.where(
        is_owner,
        MEMBERS - 1 + x + g + jnp.where(jnp.logical_and(g >= 1, has_rows), NEAR, 0),
        PIECES)

    loads[2].wait()
    loads[3].wait()
    for which, (src, dst) in enumerate(((rates_ref, dec), (res_ref, scale))):
        for b in range(M // 8):
            for j in range(LB):
                relay[which * 128 + (b * 8 + j) * 8:which * 128 + (b * 8 + j) * 8 + 8, :] = (
                    src[b * 8:b * 8 + 8, j * LANES:(j + 1) * LANES])

    def mode_rate(m):
        return relay[token_row(m // 8, m % 8), :]

    for m in range(M):
        d = jnp.exp(-mode_rate(m))
        dec[m] = d
        leap[m] = jnp.exp(-mode_rate(m) * (COUNT // SEGS))
        scale[m] = relay[pl.ds(128 + (m // 8) * 64 + m % 8, 8, stride=8), :] * jnp.sqrt(1.0 - d * d)

    loads[0].wait()
    loads[1].wait()

    def make_driven(b, _):
        rows = pl.ds(pl.multiple_of(b * 16, 16), 16)
        for j in range(LB):
            cols = slice(j * LANES, (j + 1) * LANES)
            d = k_ref[rows, cols].astype(F32) * v_ref[rows, cols].astype(F32)
            driven[pl.ds(pl.multiple_of(b * 128 + j * 8, 8), 8), :] = d[:8]
            driven[pl.ds(pl.multiple_of(b * 128 + 64 + j * 8, 8), 8), :] = d[8:]
        return 0

    lax.fori_loop(0, COUNT // 16, make_driven, 0)

    def fwd_copy(p):
        return pltpu.make_async_remote_copy(
            src_ref=ends.at[pl.ds(p * PM, PM)], dst_ref=fwd_buf.at[me],
            send_sem=fwd_send.at[p], recv_sem=fwd_recv.at[me],
            device_id=owner_device(p), device_id_type=MESH)

    pl.semaphore_wait(barrier, expected)
    earlier_y(lambda dev: ready(y_ready, dev))

    @pl.when(is_owner)
    def _():
        for src in range(NX - 1):
            @pl.when(src < x)
            def _(src=src):
                ready(x_ready, device(src, z, core, y))

        @pl.when(g >= 1)
        def _():
            ready(ex_ready, peer_owner(0))

        @pl.when(g == 2)
        def _():
            ready(ex_ready, peer_owner(1))

    order = ((1 - pair) * 2, (1 - pair) * 2 + 1, pair * 2 + 1 - core, pair * 2 + core)
    for p in order:
        decays = [dec[p * PM + i] for i in range(PM)]

        def steps(b, states, decays=decays):
            states = list(states)
            for s in range(8):
                for seg in range(SEGS):
                    d = driven[token_row(seg * SEG_BLOCKS + b, s), :]
                    for i in range(PM):
                        n = seg * PM + i
                        states[n] = states[n] * decays[i] + d
            return tuple(states)

        zero = jnp.zeros((8, LANES), F32)
        states = lax.fori_loop(0, SEG_BLOCKS, steps, (zero,) * (SEGS * PM))
        for i in range(PM):
            m = p * PM + i
            s = states[i]
            for seg in range(1, SEGS):
                s = s * leap[m] + states[seg * PM + i]
            ends[m] = s
        @pl.when(jnp.logical_not(is_me(p)))
        def _(p=p):
            fwd_copy(p).start()

    def conv_steps(b, states):
        states = list(states)
        for s in range(8):
            d = driven[token_row(b, s), :]
            terms = []
            for m in range(M):
                states[m] = states[m] * dec[m] + d
                terms.append(states[m] * scale[m])
            while len(terms) > 1:
                terms = [terms[i] + terms[i + 1] for i in range(0, len(terms), 2)]
            conv[pl.ds(pl.multiple_of(b * 64 + s * 8, 8), 8), :] = terms[0]
        return tuple(states)

    zero = jnp.zeros((8, LANES), F32)
    lax.fori_loop(0, BLOCKS, conv_steps, (zero,) * M)

    loads[4].wait()
    loads[5].wait()

    def make_base(b, _):
        rows = pl.ds(pl.multiple_of(b * 16, 16), 16)
        for j in range(LB):
            q = q_ref[rows, j * LANES:(j + 1) * LANES].astype(F32)
            gate = skip_ref[j:j + 1, :]
            for h in range(2):
                at = pl.ds(pl.multiple_of(b * 128 + h * 64 + j * 8, 8), 8)
                local = conv[pl.ds(b * 128 + h * 64 + j, 8, stride=8), :]
                base[at, :] = q[h * 8:h * 8 + 8] * (local + gate * driven[at, :])
        return 0

    lax.fori_loop(0, COUNT // 16, make_base, 0)

    def back_copy(j):
        return pltpu.make_async_remote_copy(
            src_ref=back_src.at[j], dst_ref=carry.at[my_piece],
            send_sem=back_send.at[j], recv_sem=back_recv.at[my_piece],
            device_id=member_device(j), device_id_type=MESH)

    def x_copy(k):
        return pltpu.make_async_remote_copy(
            src_ref=total, dst_ref=x_buf.at[x],
            send_sem=x_send.at[k - 1], recv_sem=x_recv.at[x],
            device_id=device(lax.rem(x + k, NX), z, core, y), device_id_type=MESH)

    def ex_copy(src, group, slot):
        return pltpu.make_async_remote_copy(
            src_ref=src, dst_ref=ex_buf.at[slot],
            send_sem=ex_send.at[slot], recv_sem=ex_recv.at[slot],
            device_id=peer_owner(group), device_id_type=MESH)

    def far_copy(j):
        return pltpu.make_async_remote_copy(
            src_ref=rows_before, dst_ref=far_buf.at[g - 1, my_piece],
            send_sem=far_send.at[j], recv_sem=far_recv.at[g - 1, my_piece],
            device_id=device(x, j // 2, j % 2, y), device_id_type=MESH)

    def far_arrival(group, p):
        return pltpu.make_async_remote_copy(
            src_ref=rows_before, dst_ref=far_buf.at[group - 1, p],
            send_sem=far_send.at[0], recv_sem=far_recv.at[group - 1, p],
            device_id=device(x, group * GROUP + OWNER_BASE[group] + lax.div(p, 2), lax.rem(p, 2), y),
            device_id_type=MESH)

    sends_far = jnp.logical_and(is_owner, jnp.logical_and(g >= 1, has_rows))
    span = COUNT * MEMBERS

    @pl.when(takes_far)
    def _():
        for m in range(M):
            rate = mode_rate(m)
            near = jnp.exp(-rate * (me * COUNT).astype(F32))
            far_coef[1, m] = near
            far_coef[0, m] = near * jnp.exp(-rate * span)

    @pl.when(is_owner)
    def _():
        for i in range(PM):
            m = my_piece * PM + i
            rate = relay[pl.ds(lax.div(m, 8) * 64 + lax.rem(m, 8), 8, stride=8), :]
            coef[0, i] = jnp.exp(-rate * COUNT)
            coef[1, i] = jnp.exp(-rate * span)
            coef[2, i] = jnp.exp(-rate * (2 * span))
            coef[3, i] = jnp.exp(-rate * (GROUPS * span))
            rows_before[i] = zero
            fwd_buf[me, i] = ends[m]
        for j in range(MEMBERS):
            @pl.when(me != j)
            def _(j=j):
                pltpu.make_async_remote_copy(
                    src_ref=ends.at[pl.ds(0, PM)], dst_ref=fwd_buf.at[j],
                    send_sem=fwd_send.at[0], recv_sem=fwd_recv.at[j],
                    device_id=member_device(j), device_id_type=MESH).wait_recv()
        for i in range(PM):
            s = fwd_buf[0, i]
            for j in range(1, MEMBERS):
                s = s * coef[0, i] + fwd_buf[j, i]
            total[i] = s
        @pl.when(x < NX - 1)
        def _():
            pl.semaphore_wait(x_ready, NX - 1 - x)

        for k in range(1, NX):
            @pl.when(x + k < NX)
            def _(k=k):
                x_copy(k).start()
        for src in range(NX - 1):
            @pl.when(src < x)
            def _(src=src):
                pltpu.make_async_remote_copy(
                    src_ref=total, dst_ref=x_buf.at[src],
                    send_sem=x_send.at[0], recv_sem=x_recv.at[src],
                    device_id=device(src, z, core, y), device_id_type=MESH).wait_recv()
                for i in range(PM):
                    rows_before[i] = rows_before[i] * coef[3, i] + x_buf[src, i]

        @pl.when(sends_far)
        def _():
            for j in range(NEAR):
                far_copy(j).start()

        for i in range(PM):
            rows_with[i] = rows_before[i] * coef[3, i] + total[i]
            start_state[i] = rows_before[i] * coef[2, i]

        @pl.when(g <= 1)
        def _():
            pl.semaphore_wait(ex_ready, 2 - g)

        @pl.when(first)
        def _():
            ex_copy(rows_with, 1, 0).start()
            ex_copy(rows_with, 2, 1).start()

        @pl.when(g == 1)
        def _():
            ex_copy(rows_with, 2, 0).start()
            ex_copy(rows_with, 0, 0).wait_recv()
            for i in range(PM):
                start_state[i] = start_state[i] + ex_buf[0, i]

            @pl.when(has_rows)
            def _():
                ex_copy(rows_before, 2, 1).wait_recv()
                for i in range(PM):
                    start_state[i] = start_state[i] + ex_buf[1, i] * coef[1, i]

        @pl.when(g == 2)
        def _():
            @pl.when(has_rows)
            def _():
                ex_copy(rows_before, 1, 1).start()

            for slot in range(2):
                ex_copy(rows_with, 1 - slot, slot).wait_recv()
            for i in range(PM):
                start_state[i] = start_state[i] + ex_buf[0, i] + ex_buf[1, i] * coef[1, i]

        def send_back(j):
            @pl.when(me != j)
            def _():
                back_copy(j).start()

            @pl.when(me == j)
            def _():
                for i in range(PM):
                    carry[my_piece, i] = back_src[j, i]

        for j in range(MEMBERS):
            for i in range(PM):
                if j == 0:
                    back_src[0, i] = start_state[i]
                else:
                    back_src[j, i] = back_src[j - 1, i] * coef[0, i] + fwd_buf[j - 1, i]
            if j < NEAR:
                send_back(j)
            else:
                @pl.when(jnp.logical_not(takes_far))
                def _(j=j):
                    send_back(j)

        @pl.when(takes_far)
        def _():
            for group in range(1, GROUPS):
                far_arrival(group, my_piece).wait_recv()
            for i in range(PM):
                far = far_buf[1, my_piece, i] + far_buf[0, my_piece, i] * coef[1, i]
                for _ in range(NEAR):
                    far = far * coef[0, i]
                for j in range(NEAR, MEMBERS):
                    back_src[j, i] = back_src[j, i] + far
                    far = far * coef[0, i]
            for j in range(NEAR, MEMBERS):
                send_back(j)

    for p in range(PIECES):
        @pl.when(jnp.logical_not(is_me(p)))
        def _(p=p):
            pltpu.make_async_remote_copy(
                src_ref=back_src.at[0], dst_ref=carry.at[p],
                send_sem=back_send.at[0], recv_sem=back_recv.at[p],
                device_id=owner_device(jnp.int32(p)), device_id_type=MESH).wait_recv()

    @pl.when(takes_far)
    def _():
        for p in range(PIECES):
            @pl.when(jnp.logical_not(is_me(p)))
            def _(p=p):
                for group in range(1, GROUPS):
                    far_arrival(group, jnp.int32(p)).wait_recv()
        for m in range(M):
            p, i = m // PM, m % PM
            carry[p, i] = carry[p, i] + far_buf[1, p, i] * far_coef[1, m] + far_buf[0, p, i] * far_coef[0, m]

    def carry_steps(b, states):
        states = list(states)
        for s in range(8):
            for m in range(M):
                states[m] = states[m] * dec[m]
            terms = states
            while len(terms) > 1:
                terms = [terms[i] + terms[i + 1] for i in range(0, len(terms), 2)]
            conv[pl.ds(pl.multiple_of(b * 64 + s * 8, 8), 8), :] = terms[0]
        return tuple(states)

    lax.fori_loop(0, BLOCKS, carry_steps,
                  tuple(carry[m // PM, m % PM] * scale[m] for m in range(M)))

    def gate_block(b, _):
        rows = pl.ds(pl.multiple_of(b * 16, 16), 16)
        sums = [jnp.zeros((8, LANES), F32)] * 2
        for j in range(LB):
            q = q_ref[rows, j * LANES:(j + 1) * LANES].astype(F32)
            for h in range(2):
                at = pl.ds(pl.multiple_of(b * 128 + h * 64 + j * 8, 8), 8)
                far = conv[pl.ds(b * 128 + h * 64 + j, 8, stride=8), :]
                gated = base[at, :] + q[h * 8:h * 8 + 8] * far
                g_ref[pl.ds(pl.multiple_of(b * 16 + h * 8, 8), 8), j * LANES:(j + 1) * LANES] = gated
                sums[h] = sums[h] + gated * gated
        squares[pl.ds(pl.multiple_of(b * 16, 8), 8), :] = sums[0]
        squares[pl.ds(pl.multiple_of(b * 16 + 8, 8), 8), :] = sums[1]
        return 0

    lax.fori_loop(0, COUNT // 16, gate_block, 0)

    weight = jnp.full((8, LANES), 1.0 / (8 * C), F32)
    part[...] = lax.dot_general(
        weight, squares[...], (((1,), (1,)), ((), ())),
        precision=lax.Precision.HIGHEST, preferred_element_type=F32)

    def y_copy(k):
        return pltpu.make_async_remote_copy(
            src_ref=part, dst_ref=parts.at[y],
            send_sem=y_send.at[k - 1], recv_sem=y_recv.at[y],
            device_id=device(x, z, core, lax.rem(y + k, NY)), device_id_type=MESH)

    @pl.when(y_rank < NY - 1)
    def _():
        pl.semaphore_wait(y_ready, NY - 1 - y_rank)

    for k in range(1, NY):
        y_copy(k).start()
    parts[y] = part[...]
    for k in range(1, NY):
        src = lax.rem(y + k, NY)
        pltpu.make_async_remote_copy(
            src_ref=part, dst_ref=parts.at[src],
            send_sem=y_send.at[0], recv_sem=y_recv.at[src],
            device_id=device(x, z, core, src), device_id_type=MESH).wait_recv()
    power = lax.dot_general(
        parts[...].reshape(NY * 8, LANES), jnp.ones((NY * 8, LANES), F32), (((0,), (0,)), ((), ())),
        precision=lax.Precision.HIGHEST, preferred_element_type=F32)
    inv_ref[...] = lax.rsqrt(power + 1e-06)

    for p in range(PIECES):
        @pl.when(jnp.logical_not(is_me(p)))
        def _(p=p):
            fwd_copy(jnp.int32(p)).wait_send()

    @pl.when(is_owner)
    def _():
        for k in range(1, NX):
            @pl.when(x + k < NX)
            def _(k=k):
                x_copy(k).wait_send()
        for j in range(MEMBERS):
            @pl.when(me != j)
            def _(j=j):
                back_copy(j).wait_send()

            if j < NEAR:
                @pl.when(sends_far)
                def _(j=j):
                    far_copy(j).wait_send()

        @pl.when(first)
        def _():
            ex_copy(rows_with, 1, 0).wait_send()
            ex_copy(rows_with, 2, 1).wait_send()

        @pl.when(g == 1)
        def _():
            ex_copy(rows_with, 2, 0).wait_send()

        @pl.when(jnp.logical_and(g == 2, has_rows))
        def _():
            ex_copy(rows_before, 1, 1).wait_send()
    for k in range(1, NY):
        y_copy(k).wait_send()


def scale_rows(g_ref, inv_ref, gain_ref, o_ref):
    def rows_of(b, _):
        rows = pl.ds(pl.multiple_of(b * 16, 16), 16)
        norm = inv_ref[rows, :]
        for j in range(LB):
            cols = slice(j * LANES, (j + 1) * LANES)
            o_ref[rows, cols] = (g_ref[rows, cols] * norm * gain_ref[j:j + 1, :]).astype(jnp.bfloat16)
        return 0

    lax.fori_loop(0, COUNT // 16, rows_of, 0)


def body(query, keys, values, rates, residues, skip, gain):
    in_vmem = lambda a: pltpu.with_memory_space_constraint(a, pltpu.VMEM)
    any_space = pl.BlockSpec(memory_space=pl.ANY)
    vmem = pltpu.VMEM
    dma = pltpu.SemaphoreType.DMA
    tile = (8, LANES)
    piece = (PM,) + tile
    gated, inv = pl.pallas_call(
        kernel,
        name="modal_scan",
        out_shape=(vmem((COUNT, WIDTH), F32), vmem((COUNT, LANES), F32)),
        in_specs=[any_space] * 6,
        out_specs=(pl.BlockSpec(memory_space=pltpu.VMEM), pl.BlockSpec(memory_space=pltpu.VMEM)),
        scratch_shapes=[
            vmem((COUNT, WIDTH), jnp.bfloat16),
            vmem((COUNT, WIDTH), jnp.bfloat16),
            vmem((COUNT, WIDTH), jnp.bfloat16),
            vmem((M, WIDTH), F32),
            vmem((M, WIDTH), F32),
            vmem(tile, F32),
            vmem((COUNT * 8, LANES), F32),
            vmem((256, LANES), F32),
            vmem((M,) + tile, F32),
            vmem((M,) + tile, F32),
            vmem((M,) + tile, F32),
            vmem((M,) + tile, F32),
            vmem((MEMBERS,) + piece, F32),
            vmem(piece, F32),
            vmem((NX,) + piece, F32),
            vmem(piece, F32),
            vmem(piece, F32),
            vmem((2,) + piece, F32),
            vmem((2, PIECES) + piece, F32),
            vmem((2, M) + tile, F32),
            vmem((4,) + piece, F32),
            vmem(piece, F32),
            vmem((MEMBERS,) + piece, F32),
            vmem((PIECES,) + piece, F32),
            vmem((COUNT * 8, LANES), F32),
            vmem((COUNT * 8, LANES), F32),
            vmem((COUNT, LANES), F32),
            vmem(tile, F32),
            vmem((NY,) + tile, F32),
            dma((6,)),
            dma((PIECES,)), dma((MEMBERS,)),
            dma((NX - 1,)), dma((NX,)),
            dma((2,)), dma((2,)),
            dma((MEMBERS,)), dma((2, PIECES)),
            dma((MEMBERS,)), dma((PIECES,)),
            dma((NY - 1,)), dma((NY,)),
            pltpu.SemaphoreType.REGULAR, pltpu.SemaphoreType.REGULAR, pltpu.SemaphoreType.REGULAR,
        ],
        compiler_params=pltpu.CompilerParams(collective_id=0, has_side_effects=True),
    )(query, keys, values, rates, residues, skip.reshape(LB, LANES))
    return pl.pallas_call(
        scale_rows,
        name="scale_rows",
        out_shape=jax.ShapeDtypeStruct((COUNT, WIDTH), jnp.bfloat16),
        in_specs=[pl.BlockSpec(memory_space=pltpu.VMEM)] * 3,
        out_specs=pl.BlockSpec(memory_space=pltpu.VMEM),
    )(in_vmem(gated), in_vmem(inv), gain.reshape(LB, LANES))


def solution(mesh):
    in_specs = (
        P("ctx", "tp"), P("ctx", "tp"), P("ctx", "tp"),
        P(None, "tp"), P(None, "tp"), P("tp"), P("tp"),
    )
    return jax.shard_map(body, mesh=mesh, in_specs=in_specs, out_specs=P("ctx", "tp"), check_vma=False)
```

```python
import jax
import jax.numpy as jnp
from jax import lax
from jax.experimental import pallas as pl
from jax.experimental.pallas import tpu as pltpu
from jax.sharding import PartitionSpec as P

MESH = pl.DeviceIdType.MESH
F32 = jnp.float32

C = 8192
NX, NZ, NY = 4, 12, 8
LANES = 128
M = 16
COUNT = 128
WIDTH = 1024
LB = WIDTH // LANES
GROUP = 4
GROUPS = NZ // GROUP
MEMBERS = 2 * GROUP
PIECES = 4
PM = M // PIECES
BLOCKS = COUNT // 8
SEGS = 4
OWNER_BASE = (0, 0, 1)
NEAR = 4
SCALE_STEPS = 1
SEG_BLOCKS = BLOCKS // SEGS


def token_row(block, s):
    return pl.ds(block * 64 + s, 8, stride=8)


def kernel(q_hbm, k_hbm, v_hbm, rates_hbm, res_hbm, skip_hbm, gain_hbm, g_ref, inv_ref,
           q_ref, k_ref, v_ref, rates_ref, res_ref, skip_ref, gain_ref,
           driven, relay, dec, scale, leap, ends, fwd_buf, total, x_buf, rows_before, rows_with,
           ex_buf, far_buf, far_coef, coef,
           start_state, back_src, carry, query, conv, base, squares, part, parts,
           in_sem, fwd_send, fwd_recv, x_send, x_recv, ex_send, ex_recv, far_send, far_recv,
           back_send, back_recv, y_send, y_recv, x_ready, ex_ready, y_ready):
    ctx = lax.axis_index("ctx")
    y = lax.axis_index("tp")
    core = lax.rem(ctx, 2)
    chip = lax.div(ctx, 2)
    z = lax.rem(chip, NZ)
    x = lax.div(chip, NZ)
    g = lax.div(z, GROUP)
    r = lax.rem(z, GROUP)
    me = r * 2 + core
    first = g == 0
    owner_base = jnp.where(g == 2, OWNER_BASE[2], OWNER_BASE[0])
    is_owner = jnp.logical_and(r >= owner_base, r <= owner_base + 1)
    offset = jnp.where(r <= owner_base, 0, 1)
    pair = jnp.where(g == 1, 1 - offset, offset)
    y_rank = jnp.where(y < NY // 2, y, NY + NY // 2 - 1 - y)
    my_piece = pair * 2 + core
    has_rows = x >= 1

    def device(dx, dz, dc, dy):
        return ((dx * NZ + dz) * 2 + dc, dy)

    def owner_device(p):
        half = lax.div(p, 2)
        return device(x, g * GROUP + owner_base + jnp.where(g == 1, 1 - half, half), lax.rem(p, 2), y)

    def owner_in(group, p):
        half = lax.div(p, 2)
        return device(x, group * GROUP + OWNER_BASE[group] + (1 - half if group == 1 else half), lax.rem(p, 2), y)

    def peer_owner(group):
        return owner_in(group, my_piece)

    def is_me(p):
        return jnp.logical_and(is_owner, my_piece == p)

    def member_device(j):
        return device(x, g * GROUP + j // 2, j % 2, y)

    loads = []
    for n, (src, dst) in enumerate((
            (k_hbm, k_ref), (v_hbm, v_ref), (rates_hbm, rates_ref), (res_hbm, res_ref),
            (q_hbm, q_ref), (skip_hbm, skip_ref), (gain_hbm, gain_ref))):
        load = pltpu.make_async_copy(src, dst, in_sem.at[n])
        load.start()
        loads.append(load)

    barrier = pltpu.get_barrier_semaphore()

    def greet(dev):
        pl.semaphore_signal(barrier, inc=1, device_id=dev, device_id_type=MESH)

    def ready(sem, dev):
        pl.semaphore_signal(sem, inc=1, device_id=dev, device_id_type=MESH)

    def earlier_y(act):
        for k in range(1, NY):
            other = lax.rem(y + k, NY)
            rank = jnp.where(other < NY // 2, other, NY + NY // 2 - 1 - other)

            @pl.when(rank < y_rank)
            def _(other=other):
                act(device(x, z, core, other))

    for p in range(PIECES):
        @pl.when(jnp.logical_not(is_me(p)))
        def _(p=p):
            greet(owner_device(jnp.int32(p)))
    for k in range(1, NY):
        other = lax.rem(y + k, NY)
        rank = jnp.where(other < NY // 2, other, NY + NY // 2 - 1 - other)

        @pl.when(rank > y_rank)
        def _(other=other):
            greet(device(x, z, core, other))

    takes_far = jnp.logical_and(jnp.logical_and(first, r < NEAR // 2), has_rows)

    @pl.when(takes_far)
    def _():
        for group in range(1, GROUPS):
            for p in range(PIECES):
                greet(owner_in(group, jnp.int32(p)))

    @pl.when(is_owner)
    def _():
        for j in range(MEMBERS):
            @pl.when(jnp.logical_or(j // 2 < owner_base, j // 2 > owner_base + 1))
            def _(j=j):
                greet(member_device(j))
        for k in range(1, NX):
            @pl.when(x + k < NX)
            def _(k=k):
                greet(device(lax.rem(x + k, NX), z, core, y))

        @pl.when(first)
        def _():
            greet(peer_owner(1))

        @pl.when(g <= 1)
        def _():
            greet(peer_owner(2))

    expected = y_rank + jnp.where(
        is_owner,
        MEMBERS - 1 + x + g + jnp.where(jnp.logical_and(g >= 1, has_rows), NEAR, 0),
        PIECES)

    loads[2].wait()
    loads[3].wait()
    for which, (src, dst) in enumerate(((rates_ref, dec), (res_ref, scale))):
        for b in range(M // 8):
            for j in range(LB):
                relay[which * 128 + (b * 8 + j) * 8:which * 128 + (b * 8 + j) * 8 + 8, :] = (
                    src[b * 8:b * 8 + 8, j * LANES:(j + 1) * LANES])

    def mode_rate(m):
        return relay[token_row(m // 8, m % 8), :]

    for m in range(M):
        d = jnp.exp(-mode_rate(m))
        dec[m] = d
        leap[m] = jnp.exp(-mode_rate(m) * (COUNT // SEGS))
        scale[m] = relay[pl.ds(128 + (m // 8) * 64 + m % 8, 8, stride=8), :] * jnp.sqrt(1.0 - d * d)

    loads[0].wait()
    loads[1].wait()

    def make_driven(b, _):
        rows = pl.ds(pl.multiple_of(b * 16, 16), 16)
        for j in range(LB):
            cols = slice(j * LANES, (j + 1) * LANES)
            d = k_ref[rows, cols].astype(F32) * v_ref[rows, cols].astype(F32)
            driven[pl.ds(pl.multiple_of(b * 128 + j * 8, 8), 8), :] = d[:8]
            driven[pl.ds(pl.multiple_of(b * 128 + 64 + j * 8, 8), 8), :] = d[8:]
        return 0

    lax.fori_loop(0, COUNT // 16, make_driven, 0)

    def fwd_copy(p):
        return pltpu.make_async_remote_copy(
            src_ref=ends.at[pl.ds(p * PM, PM)], dst_ref=fwd_buf.at[me],
            send_sem=fwd_send.at[p], recv_sem=fwd_recv.at[me],
            device_id=owner_device(p), device_id_type=MESH)

    def meet():
        pl.semaphore_wait(barrier, expected)
        earlier_y(lambda dev: ready(y_ready, dev))

        @pl.when(is_owner)
        def _():
            for src in range(NX - 1):
                @pl.when(src < x)
                def _(src=src):
                    ready(x_ready, device(src, z, core, y))

            @pl.when(g >= 1)
            def _():
                ready(ex_ready, peer_owner(0))

            @pl.when(g == 2)
            def _():
                ready(ex_ready, peer_owner(1))

    order = ((1 - pair) * 2, (1 - pair) * 2 + 1, pair * 2 + 1 - core, pair * 2 + core)
    for n_piece, p in enumerate(order):
        decays = [dec[p * PM + i] for i in range(PM)]

        def steps(b, states, decays=decays):
            states = list(states)
            for s in range(8):
                for seg in range(SEGS):
                    d = driven[token_row(seg * SEG_BLOCKS + b, s), :]
                    for i in range(PM):
                        n = seg * PM + i
                        states[n] = states[n] * decays[i] + d
            return tuple(states)

        zero = jnp.zeros((8, LANES), F32)
        states = lax.fori_loop(0, SEG_BLOCKS, steps, (zero,) * (SEGS * PM))
        for i in range(PM):
            m = p * PM + i
            s = states[i]
            for seg in range(1, SEGS):
                s = s * leap[m] + states[seg * PM + i]
            ends[m] = s
        if n_piece == 1:
            meet()
        if n_piece >= 1:
            for ready_piece in order[0 if n_piece == 1 else n_piece:n_piece + 1]:
                @pl.when(jnp.logical_not(is_me(ready_piece)))
                def _(p=ready_piece):
                    fwd_copy(p).start()

    loads[4].wait()
    loads[5].wait()
    loads[6].wait()

    def make_query(b, _):
        rows = pl.ds(pl.multiple_of(b * 16, 16), 16)
        for j in range(LB):
            q = q_ref[rows, j * LANES:(j + 1) * LANES].astype(F32)
            query[pl.ds(pl.multiple_of(b * 128 + j * 8, 8), 8), :] = q[:8]
            query[pl.ds(pl.multiple_of(b * 128 + 64 + j * 8, 8), 8), :] = q[8:]
        return 0

    lax.fori_loop(0, COUNT // 16, make_query, 0)

    def tree_sum(terms):
        while len(terms) > 1:
            terms = [terms[i] + terms[i + 1] for i in range(0, len(terms), 2)]
        return terms[0]

    def conv_steps(b, states):
        states = list(states)
        for s in range(8):
            d = driven[token_row(b, s), :]
            terms = []
            for m in range(M):
                states[m] = states[m] * dec[m] + d
                terms.append(states[m] * scale[m])
            local = tree_sum(terms) + skip_ref[...] * d
            base[pl.ds(pl.multiple_of(b * 64 + s * 8, 8), 8), :] = query[token_row(b, s), :] * local
        return tuple(states)

    zero = jnp.zeros((8, LANES), F32)
    lax.fori_loop(0, BLOCKS, conv_steps, (zero,) * M)

    def back_copy(j):
        return pltpu.make_async_remote_copy(
            src_ref=back_src.at[j], dst_ref=carry.at[my_piece],
            send_sem=back_send.at[j], recv_sem=back_recv.at[my_piece],
            device_id=member_device(j), device_id_type=MESH)

    def x_copy(k):
        return pltpu.make_async_remote_copy(
            src_ref=total, dst_ref=x_buf.at[x],
            send_sem=x_send.at[k - 1], recv_sem=x_recv.at[x],
            device_id=device(lax.rem(x + k, NX), z, core, y), device_id_type=MESH)

    def ex_copy(src, group, slot):
        return pltpu.make_async_remote_copy(
            src_ref=src, dst_ref=ex_buf.at[slot],
            send_sem=ex_send.at[slot], recv_sem=ex_recv.at[slot],
            device_id=peer_owner(group), device_id_type=MESH)

    def far_copy(j):
        return pltpu.make_async_remote_copy(
            src_ref=rows_before, dst_ref=far_buf.at[g - 1, my_piece],
            send_sem=far_send.at[j], recv_sem=far_recv.at[g - 1, my_piece],
            device_id=device(x, j // 2, j % 2, y), device_id_type=MESH)

    def far_arrival(group, p):
        return pltpu.make_async_remote_copy(
            src_ref=rows_before, dst_ref=far_buf.at[group - 1, p],
            send_sem=far_send.at[0], recv_sem=far_recv.at[group - 1, p],
            device_id=owner_in(group, p),
            device_id_type=MESH)

    sends_far = jnp.logical_and(is_owner, jnp.logical_and(g >= 1, has_rows))
    span = COUNT * MEMBERS

    @pl.when(takes_far)
    def _():
        for m in range(M):
            rate = mode_rate(m)
            near = jnp.exp(-rate * (me * COUNT).astype(F32))
            far_coef[1, m] = near
            far_coef[0, m] = near * jnp.exp(-rate * span)

    @pl.when(is_owner)
    def _():
        for i in range(PM):
            m = my_piece * PM + i
            rate = relay[pl.ds(lax.div(m, 8) * 64 + lax.rem(m, 8), 8, stride=8), :]
            coef[0, i] = jnp.exp(-rate * COUNT)
            coef[1, i] = jnp.exp(-rate * span)
            coef[2, i] = jnp.exp(-rate * (2 * span))
            coef[3, i] = jnp.exp(-rate * (GROUPS * span))
            rows_before[i] = zero
            fwd_buf[me, i] = ends[m]
        for j in range(MEMBERS):
            @pl.when(me != j)
            def _(j=j):
                pltpu.make_async_remote_copy(
                    src_ref=ends.at[pl.ds(0, PM)], dst_ref=fwd_buf.at[j],
                    send_sem=fwd_send.at[0], recv_sem=fwd_recv.at[j],
                    device_id=member_device(j), device_id_type=MESH).wait_recv()
        for i in range(PM):
            s = fwd_buf[0, i]
            for j in range(1, MEMBERS):
                s = s * coef[0, i] + fwd_buf[j, i]
            total[i] = s
        @pl.when(x < NX - 1)
        def _():
            pl.semaphore_wait(x_ready, NX - 1 - x)

        for k in range(1, NX):
            @pl.when(x + k < NX)
            def _(k=k):
                x_copy(k).start()
        for src in range(NX - 1):
            @pl.when(src < x)
            def _(src=src):
                pltpu.make_async_remote_copy(
                    src_ref=total, dst_ref=x_buf.at[src],
                    send_sem=x_send.at[0], recv_sem=x_recv.at[src],
                    device_id=device(src, z, core, y), device_id_type=MESH).wait_recv()
                for i in range(PM):
                    rows_before[i] = rows_before[i] * coef[3, i] + x_buf[src, i]

        for j in range(NEAR):
            @pl.when(jnp.logical_and(sends_far, my_piece == j))
            def _(j=j):
                far_copy(j).start()

        for i in range(PM):
            rows_with[i] = rows_before[i] * coef[3, i] + total[i]
            start_state[i] = rows_before[i] * coef[2, i]

        @pl.when(g == 1)
        def _():
            pl.semaphore_wait(ex_ready, 1)
            ex_copy(rows_with, 2, 0).start()

        for j in range(NEAR):
            @pl.when(jnp.logical_and(sends_far, my_piece != j))
            def _(j=j):
                far_copy(j).start()

        @pl.when(jnp.logical_and(g == 2, has_rows))
        def _():
            ex_copy(rows_before, 1, 1).start()

        @pl.when(g == 1)
        def _():
            ex_copy(rows_with, 0, 0).wait_recv()
            for i in range(PM):
                start_state[i] = start_state[i] + ex_buf[0, i]

            @pl.when(has_rows)
            def _():
                ex_copy(rows_before, 2, 1).wait_recv()
                for i in range(PM):
                    start_state[i] = start_state[i] + ex_buf[1, i] * coef[1, i]

        @pl.when(g == 2)
        def _():
            for slot in range(2):
                ex_copy(rows_with, 1 - slot, slot).wait_recv()
            for i in range(PM):
                start_state[i] = start_state[i] + ex_buf[0, i] + ex_buf[1, i] * coef[1, i]

        def send_back(j):
            @pl.when(me != j)
            def _():
                back_copy(j).start()

            @pl.when(me == j)
            def _():
                for i in range(PM):
                    carry[my_piece, i] = back_src[j, i]

        for j in range(MEMBERS):
            for i in range(PM):
                if j == 0:
                    back_src[0, i] = start_state[i]
                else:
                    back_src[j, i] = back_src[j - 1, i] * coef[0, i] + fwd_buf[j - 1, i]
            if j < NEAR:
                send_back(j)
            else:
                @pl.when(jnp.logical_not(takes_far))
                def _(j=j):
                    send_back(j)

        @pl.when(first)
        def _():
            pl.semaphore_wait(ex_ready, 2)
            ex_copy(rows_with, 1, 0).start()
            ex_copy(rows_with, 2, 1).start()

    def serve_behind():
        for group in range(1, GROUPS):
            far_arrival(group, my_piece).wait_recv()
        for i in range(PM):
            far = far_buf[1, my_piece, i] + far_buf[0, my_piece, i] * coef[1, i]
            for _ in range(NEAR):
                far = far * coef[0, i]
            for j in range(NEAR, MEMBERS):
                back_src[j, i] = back_src[j, i] + far
                far = far * coef[0, i]
        for j in range(NEAR, MEMBERS):
            back_copy(j).start()

    def take(p):
        @pl.when(jnp.logical_not(is_me(p)))
        def _():
            pltpu.make_async_remote_copy(
                src_ref=back_src.at[0], dst_ref=carry.at[p],
                send_sem=back_send.at[0], recv_sem=back_recv.at[p],
                device_id=owner_device(jnp.int32(p)), device_id_type=MESH).wait_recv()

    def take_far(p):
        @pl.when(jnp.logical_not(is_me(p)))
        def _():
            for group in range(1, GROUPS):
                far_arrival(group, jnp.int32(p)).wait_recv()

    def add_far(p):
        for i in range(PM):
            m = p * PM + i
            carry[p, i] = carry[p, i] + far_buf[1, p, i] * far_coef[1, m] + far_buf[0, p, i] * far_coef[0, m]

    near_owner = jnp.logical_and(is_owner, takes_far)

    def collect(pieces):
        for p in pieces:
            take(p)

        @pl.when(takes_far)
        def _():
            for p in pieces:
                take_far(p)
            for p in pieces:
                add_far(p)

    def first_steps(b, states):
        states = list(states)
        for s in range(8):
            for n in range(M // 2):
                states[n] = states[n] * dec[M // 2 + n]
            conv[pl.ds(pl.multiple_of(b * 64 + s * 8, 8), 8), :] = tree_sum(states)
        return tuple(states)

    def last_steps(b, states):
        states = list(states)
        for s in range(8):
            for m in range(M // 2):
                states[m] = states[m] * dec[m]
            at = pl.ds(pl.multiple_of(b * 64 + s * 8, 8), 8)
            gated = base[at, :] + query[token_row(b, s), :] * (conv[at, :] + tree_sum(states))
            base[at, :] = gated
            conv[at, :] = gated * gated
        rows = [conv[token_row(b, s), :] for s in range(8)]
        squares[pl.ds(pl.multiple_of(b * 8, 8), 8), :] = tree_sum(rows)
        return tuple(states)

    def starts(pieces):
        return tuple(carry[p, i] * scale[p * PM + i] for p in pieces for i in range(PM))

    @pl.when(near_owner)
    def _():
        serve_behind()

    collect((2, 3))
    lax.fori_loop(0, BLOCKS, first_steps, starts((2, 3)))
    collect((0, 1))
    lax.fori_loop(0, BLOCKS, last_steps, starts((0, 1)))

    def exact_dot(a, b, dims):
        return lax.dot_general(a, b, (dims, ((), ())), preferred_element_type=F32)

    def split(a):
        high = a.astype(jnp.bfloat16)
        return high, (a - high.astype(F32)).astype(jnp.bfloat16)

    weight = jnp.full((8, LANES), 1.0 / (8 * C), jnp.bfloat16)
    high, low = split(squares[...])
    part[...] = exact_dot(weight, high, ((1,), (1,))) + exact_dot(weight, low, ((1,), (1,)))

    def y_copy(k):
        return pltpu.make_async_remote_copy(
            src_ref=part, dst_ref=parts.at[y],
            send_sem=y_send.at[k - 1], recv_sem=y_recv.at[y],
            device_id=device(x, z, core, lax.rem(y + k, NY)), device_id_type=MESH)

    @pl.when(y_rank < NY - 1)
    def _():
        pl.semaphore_wait(y_ready, NY - 1 - y_rank)

    for k in (4, 3, 5, 2, 6, 1, 7):
        y_copy(k).start()
    parts[y] = part[...]

    def relayout(b, _):
        rows = pl.ds(pl.multiple_of(b * 8, 8), 8)
        for j in range(LB):
            g_ref[rows, j * LANES:(j + 1) * LANES] = base[token_row(b, j), :] * gain_ref[j:j + 1, :]
        return 0

    lax.fori_loop(0, BLOCKS, relayout, 0)
    for k in range(1, NY):
        src = lax.rem(y + k, NY)
        pltpu.make_async_remote_copy(
            src_ref=part, dst_ref=parts.at[src],
            send_sem=y_send.at[0], recv_sem=y_recv.at[src],
            device_id=device(x, z, core, src), device_id_type=MESH).wait_recv()
    unit = jnp.ones((NY * 8, LANES), jnp.bfloat16)
    high, low = split(parts[...].reshape(NY * 8, LANES))
    power = exact_dot(high, unit, ((0,), (0,))) + exact_dot(low, unit, ((0,), (0,)))
    inv_ref[...] = lax.rsqrt(power + 1e-06)

    for p in range(PIECES):
        @pl.when(jnp.logical_not(is_me(p)))
        def _(p=p):
            fwd_copy(jnp.int32(p)).wait_send()

    @pl.when(is_owner)
    def _():
        for k in range(1, NX):
            @pl.when(x + k < NX)
            def _(k=k):
                x_copy(k).wait_send()
        for j in range(MEMBERS):
            @pl.when(me != j)
            def _(j=j):
                back_copy(j).wait_send()

            if j < NEAR:
                @pl.when(sends_far)
                def _(j=j):
                    far_copy(j).wait_send()

        @pl.when(first)
        def _():
            ex_copy(rows_with, 1, 0).wait_send()
            ex_copy(rows_with, 2, 1).wait_send()

        @pl.when(g == 1)
        def _():
            ex_copy(rows_with, 2, 0).wait_send()

        @pl.when(jnp.logical_and(g == 2, has_rows))
        def _():
            ex_copy(rows_before, 1, 1).wait_send()
    for k in range(1, NY):
        y_copy(k).wait_send()


def scale_rows(g_ref, inv_ref, o_ref):
    height = COUNT // SCALE_STEPS
    top = pl.program_id(0) * height

    def rows_of(b, _):
        rows = pl.ds(pl.multiple_of(top + b * 16, 16), 16)
        norm = inv_ref[rows, :]
        for j in range(LB):
            cols = slice(j * LANES, (j + 1) * LANES)
            o_ref[pl.ds(pl.multiple_of(b * 16, 16), 16), cols] = (g_ref[rows, cols] * norm).astype(jnp.bfloat16)
        return 0

    lax.fori_loop(0, height // 16, rows_of, 0)


def body(query, keys, values, rates, residues, skip, gain):
    in_vmem = lambda a: pltpu.with_memory_space_constraint(a, pltpu.VMEM)
    any_space = pl.BlockSpec(memory_space=pl.ANY)
    vmem = pltpu.VMEM
    dma = pltpu.SemaphoreType.DMA
    tile = (8, LANES)
    piece = (PM,) + tile
    gated, inv = pl.pallas_call(
        kernel,
        name="modal_scan",
        out_shape=(vmem((COUNT, WIDTH), F32), vmem((COUNT, LANES), F32)),
        in_specs=[any_space] * 7,
        out_specs=(pl.BlockSpec(memory_space=pltpu.VMEM), pl.BlockSpec(memory_space=pltpu.VMEM)),
        scratch_shapes=[
            vmem((COUNT, WIDTH), jnp.bfloat16),
            vmem((COUNT, WIDTH), jnp.bfloat16),
            vmem((COUNT, WIDTH), jnp.bfloat16),
            vmem((M, WIDTH), F32),
            vmem((M, WIDTH), F32),
            vmem(tile, F32),
            vmem(tile, F32),
            vmem((COUNT * 8, LANES), F32),
            vmem((256, LANES), F32),
            vmem((M,) + tile, F32),
            vmem((M,) + tile, F32),
            vmem((M,) + tile, F32),
            vmem((M,) + tile, F32),
            vmem((MEMBERS,) + piece, F32),
            vmem(piece, F32),
            vmem((NX,) + piece, F32),
            vmem(piece, F32),
            vmem(piece, F32),
            vmem((2,) + piece, F32),
            vmem((2, PIECES) + piece, F32),
            vmem((2, M) + tile, F32),
            vmem((4,) + piece, F32),
            vmem(piece, F32),
            vmem((MEMBERS,) + piece, F32),
            vmem((PIECES,) + piece, F32),
            vmem((COUNT * 8, LANES), F32),
            vmem((COUNT * 8, LANES), F32),
            vmem((COUNT * 8, LANES), F32),
            vmem((COUNT, LANES), F32),
            vmem(tile, F32),
            vmem((NY,) + tile, F32),
            dma((7,)),
            dma((PIECES,)), dma((MEMBERS,)),
            dma((NX - 1,)), dma((NX,)),
            dma((2,)), dma((2,)),
            dma((MEMBERS,)), dma((2, PIECES)),
            dma((MEMBERS,)), dma((PIECES,)),
            dma((NY - 1,)), dma((NY,)),
            pltpu.SemaphoreType.REGULAR, pltpu.SemaphoreType.REGULAR, pltpu.SemaphoreType.REGULAR,
        ],
        compiler_params=pltpu.CompilerParams(collective_id=0, has_side_effects=True),
    )(query, keys, values, rates, residues, skip.reshape(LB, LANES), gain.reshape(LB, LANES))
    return pl.pallas_call(
        scale_rows,
        name="scale_rows",
        out_shape=jax.ShapeDtypeStruct((COUNT, WIDTH), jnp.bfloat16),
        grid=(SCALE_STEPS,),
        in_specs=[pl.BlockSpec(memory_space=pltpu.VMEM)] * 2,
        out_specs=pl.BlockSpec((COUNT // SCALE_STEPS, WIDTH), lambda n: (n, 0)),
    )(in_vmem(gated), in_vmem(inv))


def solution(mesh):
    in_specs = (
        P("ctx", "tp"), P("ctx", "tp"), P("ctx", "tp"),
        P(None, "tp"), P(None, "tp"), P("tp"), P("tp"),
    )
    return jax.shard_map(body, mesh=mesh, in_specs=in_specs, out_specs=P("ctx", "tp"), check_vma=False)
```

```python
import jax
import jax.numpy as jnp
from jax import lax
from jax.experimental import pallas as pl
from jax.experimental.pallas import tpu as pltpu
from jax.sharding import PartitionSpec as P

MESH = pl.DeviceIdType.MESH
F32 = jnp.float32

C = 8192
NX, NZ, NY = 4, 12, 8
LANES = 128
M = 16
COUNT = 128
WIDTH = 1024
LB = WIDTH // LANES
GROUP = 4
GROUPS = NZ // GROUP
MEMBERS = 2 * GROUP
PIECES = 4
PM = M // PIECES
BLOCKS = COUNT // 8
SEGS = 4
OWNER_BASE = (0, 0, 1)
NEAR = 4
SCALE_STEPS = 4
SEG_BLOCKS = BLOCKS // SEGS


def token_row(block, s):
    return pl.ds(block * 64 + s, 8, stride=8)


def kernel(q_hbm, k_hbm, v_hbm, rates_hbm, res_hbm, skip_hbm, gain_hbm, g_ref, inv_ref,
           q_ref, k_ref, v_ref, rates_ref, res_ref, skip_ref, gain_ref,
           driven, relay, dec, scale, leap, ends, fwd_buf, total, x_buf, rows_before, rows_with,
           ex_buf, far_buf, far_coef, coef,
           start_state, back_src, carry, query, conv, base, squares, part, parts,
           in_sem, fwd_send, fwd_recv, x_send, x_recv, ex_send, ex_recv, far_send, far_recv,
           back_send, back_recv, y_send, y_recv, x_ready, ex_ready, y_ready):
    ctx = lax.axis_index("ctx")
    y = lax.axis_index("tp")
    core = lax.rem(ctx, 2)
    chip = lax.div(ctx, 2)
    z = lax.rem(chip, NZ)
    x = lax.div(chip, NZ)
    g = lax.div(z, GROUP)
    r = lax.rem(z, GROUP)
    me = r * 2 + core
    first = g == 0
    owner_base = jnp.where(g == 2, OWNER_BASE[2], OWNER_BASE[0])
    is_owner = jnp.logical_and(r >= owner_base, r <= owner_base + 1)
    offset = jnp.where(r <= owner_base, 0, 1)
    pair = jnp.where(g == 1, 1 - offset, offset)
    y_rank = jnp.where(y < NY // 2, y, NY + NY // 2 - 1 - y)
    my_piece = pair * 2 + core
    has_rows = x >= 1

    def device(dx, dz, dc, dy):
        return ((dx * NZ + dz) * 2 + dc, dy)

    def owner_device(p):
        half = lax.div(p, 2)
        return device(x, g * GROUP + owner_base + jnp.where(g == 1, 1 - half, half), lax.rem(p, 2), y)

    def owner_in(group, p):
        half = lax.div(p, 2)
        return device(x, group * GROUP + OWNER_BASE[group] + (1 - half if group == 1 else half), lax.rem(p, 2), y)

    def peer_owner(group):
        return owner_in(group, my_piece)

    def is_me(p):
        return jnp.logical_and(is_owner, my_piece == p)

    def member_device(j):
        return device(x, g * GROUP + j // 2, j % 2, y)

    loads = []
    for n, (src, dst) in enumerate((
            (k_hbm, k_ref), (v_hbm, v_ref), (rates_hbm, rates_ref), (res_hbm, res_ref),
            (q_hbm, q_ref), (skip_hbm, skip_ref), (gain_hbm, gain_ref))):
        load = pltpu.make_async_copy(src, dst, in_sem.at[n])
        load.start()
        loads.append(load)

    barrier = pltpu.get_barrier_semaphore()

    def greet(dev):
        pl.semaphore_signal(barrier, inc=1, device_id=dev, device_id_type=MESH)

    def ready(sem, dev):
        pl.semaphore_signal(sem, inc=1, device_id=dev, device_id_type=MESH)

    def earlier_y(act):
        for k in range(1, NY):
            other = lax.rem(y + k, NY)
            rank = jnp.where(other < NY // 2, other, NY + NY // 2 - 1 - other)

            @pl.when(rank < y_rank)
            def _(other=other):
                act(device(x, z, core, other))

    for p in range(PIECES):
        @pl.when(jnp.logical_not(is_me(p)))
        def _(p=p):
            greet(owner_device(jnp.int32(p)))
    for k in range(1, NY):
        other = lax.rem(y + k, NY)
        rank = jnp.where(other < NY // 2, other, NY + NY // 2 - 1 - other)

        @pl.when(rank > y_rank)
        def _(other=other):
            greet(device(x, z, core, other))

    takes_far = jnp.logical_and(jnp.logical_and(first, r < NEAR // 2), has_rows)

    @pl.when(takes_far)
    def _():
        for group in range(1, GROUPS):
            for p in range(PIECES):
                greet(owner_in(group, jnp.int32(p)))

    @pl.when(is_owner)
    def _():
        for j in range(MEMBERS):
            @pl.when(jnp.logical_or(j // 2 < owner_base, j // 2 > owner_base + 1))
            def _(j=j):
                greet(member_device(j))
        for k in range(1, NX):
            @pl.when(x + k < NX)
            def _(k=k):
                greet(device(lax.rem(x + k, NX), z, core, y))

        @pl.when(first)
        def _():
            greet(peer_owner(1))

        @pl.when(g <= 1)
        def _():
            greet(peer_owner(2))

    expected = y_rank + jnp.where(
        is_owner,
        MEMBERS - 1 + x + g + jnp.where(jnp.logical_and(g >= 1, has_rows), NEAR, 0),
        PIECES)

    loads[2].wait()
    loads[3].wait()
    for which, (src, dst) in enumerate(((rates_ref, dec), (res_ref, scale))):
        for b in range(M // 8):
            for j in range(LB):
                relay[which * 128 + (b * 8 + j) * 8:which * 128 + (b * 8 + j) * 8 + 8, :] = (
                    src[b * 8:b * 8 + 8, j * LANES:(j + 1) * LANES])

    def mode_rate(m):
        return relay[token_row(m // 8, m % 8), :]

    for m in range(M):
        d = jnp.exp(-mode_rate(m))
        dec[m] = d
        leap[m] = jnp.exp(-mode_rate(m) * (COUNT // SEGS))
        scale[m] = relay[pl.ds(128 + (m // 8) * 64 + m % 8, 8, stride=8), :] * jnp.sqrt(1.0 - d * d)

    loads[0].wait()
    loads[1].wait()

    def make_driven(b, _):
        rows = pl.ds(pl.multiple_of(b * 16, 16), 16)
        for j in range(LB):
            cols = slice(j * LANES, (j + 1) * LANES)
            d = k_ref[rows, cols].astype(F32) * v_ref[rows, cols].astype(F32)
            driven[pl.ds(pl.multiple_of(b * 128 + j * 8, 8), 8), :] = d[:8]
            driven[pl.ds(pl.multiple_of(b * 128 + 64 + j * 8, 8), 8), :] = d[8:]
        return 0

    lax.fori_loop(0, COUNT // 16, make_driven, 0)

    def fwd_copy(p):
        return pltpu.make_async_remote_copy(
            src_ref=ends.at[pl.ds(p * PM, PM)], dst_ref=fwd_buf.at[me],
            send_sem=fwd_send.at[p], recv_sem=fwd_recv.at[me],
            device_id=owner_device(p), device_id_type=MESH)

    def answer_rows():
        @pl.when(is_owner)
        def _():
            for src in range(NX - 1):
                @pl.when(src < x)
                def _(src=src):
                    ready(x_ready, device(src, z, core, y))

    def answer():
        earlier_y(lambda dev: ready(y_ready, dev))

        @pl.when(jnp.logical_and(is_owner, g >= 1))
        def _():
            ready(ex_ready, peer_owner(0))

        @pl.when(jnp.logical_and(is_owner, g == 2))
        def _():
            ready(ex_ready, peer_owner(1))

    order = ((1 - pair) * 2, (1 - pair) * 2 + 1, pair * 2 + 1 - core, pair * 2 + core)
    for n_piece, p in enumerate(order):
        decays = [dec[p * PM + i] for i in range(PM)]

        def steps(b, states, decays=decays):
            states = list(states)
            for s in range(8):
                for seg in range(SEGS):
                    d = driven[token_row(seg * SEG_BLOCKS + b, s), :]
                    for i in range(PM):
                        n = seg * PM + i
                        states[n] = states[n] * decays[i] + d
            return tuple(states)

        zero = jnp.zeros((8, LANES), F32)
        states = lax.fori_loop(0, SEG_BLOCKS, steps, (zero,) * (SEGS * PM))
        for i in range(PM):
            m = p * PM + i
            s = states[i]
            for seg in range(1, SEGS):
                s = s * leap[m] + states[seg * PM + i]
            ends[m] = s
        if n_piece == 1:
            pl.semaphore_wait(barrier, expected)
        if n_piece >= 1:
            for ready_piece in order[0 if n_piece == 1 else n_piece:n_piece + 1]:
                @pl.when(jnp.logical_not(is_me(ready_piece)))
                def _(p=ready_piece):
                    fwd_copy(p).start()
        if n_piece == 1:
            answer_rows()
    answer()

    loads[4].wait()
    loads[5].wait()
    loads[6].wait()

    def make_query(b, _):
        rows = pl.ds(pl.multiple_of(b * 16, 16), 16)
        for j in range(LB):
            q = q_ref[rows, j * LANES:(j + 1) * LANES].astype(F32)
            query[pl.ds(pl.multiple_of(b * 128 + j * 8, 8), 8), :] = q[:8]
            query[pl.ds(pl.multiple_of(b * 128 + 64 + j * 8, 8), 8), :] = q[8:]
        return 0

    lax.fori_loop(0, COUNT // 16, make_query, 0)

    def tree_sum(terms):
        while len(terms) > 1:
            terms = [terms[i] + terms[i + 1] for i in range(0, len(terms), 2)]
        return terms[0]

    def conv_steps(b, states):
        states = list(states)
        for s in range(8):
            d = driven[token_row(b, s), :]
            terms = []
            for m in range(M):
                states[m] = states[m] * dec[m] + d
                terms.append(states[m] * scale[m])
            local = tree_sum(terms) + skip_ref[...] * d
            base[pl.ds(pl.multiple_of(b * 64 + s * 8, 8), 8), :] = query[token_row(b, s), :] * local
        return tuple(states)

    zero = jnp.zeros((8, LANES), F32)
    lax.fori_loop(0, BLOCKS, conv_steps, (zero,) * M)

    def back_copy(j):
        return pltpu.make_async_remote_copy(
            src_ref=back_src.at[j], dst_ref=carry.at[my_piece],
            send_sem=back_send.at[j], recv_sem=back_recv.at[my_piece],
            device_id=member_device(j), device_id_type=MESH)

    def x_copy(k):
        return pltpu.make_async_remote_copy(
            src_ref=total, dst_ref=x_buf.at[x],
            send_sem=x_send.at[k - 1], recv_sem=x_recv.at[x],
            device_id=device(lax.rem(x + k, NX), z, core, y), device_id_type=MESH)

    def ex_copy(src, group, slot):
        return pltpu.make_async_remote_copy(
            src_ref=src, dst_ref=ex_buf.at[slot],
            send_sem=ex_send.at[slot], recv_sem=ex_recv.at[slot],
            device_id=peer_owner(group), device_id_type=MESH)

    def far_copy(j):
        return pltpu.make_async_remote_copy(
            src_ref=rows_before, dst_ref=far_buf.at[g - 1, my_piece],
            send_sem=far_send.at[j], recv_sem=far_recv.at[g - 1, my_piece],
            device_id=device(x, j // 2, j % 2, y), device_id_type=MESH)

    def far_arrival(group, p):
        return pltpu.make_async_remote_copy(
            src_ref=rows_before, dst_ref=far_buf.at[group - 1, p],
            send_sem=far_send.at[0], recv_sem=far_recv.at[group - 1, p],
            device_id=owner_in(group, p),
            device_id_type=MESH)

    sends_far = jnp.logical_and(is_owner, jnp.logical_and(g >= 1, has_rows))
    span = COUNT * MEMBERS

    @pl.when(takes_far)
    def _():
        for m in range(M):
            rate = mode_rate(m)
            near = jnp.exp(-rate * (me * COUNT).astype(F32))
            far_coef[1, m] = near
            far_coef[0, m] = near * jnp.exp(-rate * span)

    @pl.when(is_owner)
    def _():
        for i in range(PM):
            m = my_piece * PM + i
            rate = relay[pl.ds(lax.div(m, 8) * 64 + lax.rem(m, 8), 8, stride=8), :]
            coef[0, i] = jnp.exp(-rate * COUNT)
            coef[1, i] = jnp.exp(-rate * span)
            coef[2, i] = jnp.exp(-rate * (2 * span))
            coef[3, i] = jnp.exp(-rate * (GROUPS * span))
            rows_before[i] = zero
            fwd_buf[me, i] = ends[m]
        for j in range(MEMBERS):
            @pl.when(me != j)
            def _(j=j):
                pltpu.make_async_remote_copy(
                    src_ref=ends.at[pl.ds(0, PM)], dst_ref=fwd_buf.at[j],
                    send_sem=fwd_send.at[0], recv_sem=fwd_recv.at[j],
                    device_id=member_device(j), device_id_type=MESH).wait_recv()
        for i in range(PM):
            s = fwd_buf[0, i]
            for j in range(1, MEMBERS):
                s = s * coef[0, i] + fwd_buf[j, i]
            total[i] = s
        @pl.when(x < NX - 1)
        def _():
            pl.semaphore_wait(x_ready, NX - 1 - x)

        for k in range(1, NX):
            @pl.when(x + k < NX)
            def _(k=k):
                x_copy(k).start()
        for src in range(NX - 1):
            @pl.when(src < x)
            def _(src=src):
                pltpu.make_async_remote_copy(
                    src_ref=total, dst_ref=x_buf.at[src],
                    send_sem=x_send.at[0], recv_sem=x_recv.at[src],
                    device_id=device(src, z, core, y), device_id_type=MESH).wait_recv()
                for i in range(PM):
                    rows_before[i] = rows_before[i] * coef[3, i] + x_buf[src, i]

        for j in range(NEAR):
            @pl.when(jnp.logical_and(sends_far, my_piece == j))
            def _(j=j):
                far_copy(j).start()

        for i in range(PM):
            rows_with[i] = rows_before[i] * coef[3, i] + total[i]
            start_state[i] = rows_before[i] * coef[2, i]

        @pl.when(g == 1)
        def _():
            pl.semaphore_wait(ex_ready, 1)
            ex_copy(rows_with, 2, 0).start()

        for j in range(NEAR):
            @pl.when(jnp.logical_and(sends_far, my_piece != j))
            def _(j=j):
                far_copy(j).start()

        @pl.when(jnp.logical_and(g == 2, has_rows))
        def _():
            ex_copy(rows_before, 1, 1).start()

        @pl.when(g == 1)
        def _():
            ex_copy(rows_with, 0, 0).wait_recv()
            for i in range(PM):
                start_state[i] = start_state[i] + ex_buf[0, i]

            @pl.when(has_rows)
            def _():
                ex_copy(rows_before, 2, 1).wait_recv()
                for i in range(PM):
                    start_state[i] = start_state[i] + ex_buf[1, i] * coef[1, i]

        @pl.when(g == 2)
        def _():
            for slot in range(2):
                ex_copy(rows_with, 1 - slot, slot).wait_recv()
            for i in range(PM):
                start_state[i] = start_state[i] + ex_buf[0, i] + ex_buf[1, i] * coef[1, i]

        def send_back(j):
            @pl.when(me != j)
            def _():
                back_copy(j).start()

            @pl.when(me == j)
            def _():
                for i in range(PM):
                    carry[my_piece, i] = back_src[j, i]

        for j in range(MEMBERS):
            for i in range(PM):
                if j == 0:
                    back_src[0, i] = start_state[i]
                else:
                    back_src[j, i] = back_src[j - 1, i] * coef[0, i] + fwd_buf[j - 1, i]
            if j < NEAR:
                send_back(j)
            else:
                @pl.when(jnp.logical_not(takes_far))
                def _(j=j):
                    send_back(j)

        @pl.when(first)
        def _():
            pl.semaphore_wait(ex_ready, 2)
            ex_copy(rows_with, 1, 0).start()
            ex_copy(rows_with, 2, 1).start()

    def serve_behind():
        for group in range(1, GROUPS):
            far_arrival(group, my_piece).wait_recv()
        for i in range(PM):
            far = far_buf[1, my_piece, i] + far_buf[0, my_piece, i] * coef[1, i]
            for _ in range(NEAR):
                far = far * coef[0, i]
            for j in range(NEAR, MEMBERS):
                back_src[j, i] = back_src[j, i] + far
                far = far * coef[0, i]
        for j in range(NEAR, MEMBERS):
            back_copy(j).start()

    def take(p):
        @pl.when(jnp.logical_not(is_me(p)))
        def _():
            pltpu.make_async_remote_copy(
                src_ref=back_src.at[0], dst_ref=carry.at[p],
                send_sem=back_send.at[0], recv_sem=back_recv.at[p],
                device_id=owner_device(jnp.int32(p)), device_id_type=MESH).wait_recv()

    def take_far(p):
        @pl.when(jnp.logical_not(is_me(p)))
        def _():
            for group in range(1, GROUPS):
                far_arrival(group, jnp.int32(p)).wait_recv()

    def add_far(p):
        for i in range(PM):
            m = p * PM + i
            carry[p, i] = carry[p, i] + far_buf[1, p, i] * far_coef[1, m] + far_buf[0, p, i] * far_coef[0, m]

    near_owner = jnp.logical_and(is_owner, takes_far)

    def collect(pieces):
        for p in pieces:
            take(p)

        @pl.when(takes_far)
        def _():
            for p in pieces:
                take_far(p)
            for p in pieces:
                add_far(p)

    def first_steps(b, states):
        states = list(states)
        for s in range(8):
            for n in range(M // 2):
                states[n] = states[n] * dec[M // 2 + n]
            conv[pl.ds(pl.multiple_of(b * 64 + s * 8, 8), 8), :] = tree_sum(states)
        return tuple(states)

    def last_steps(b, states):
        states = list(states)
        for s in range(8):
            for m in range(M // 2):
                states[m] = states[m] * dec[m]
            at = pl.ds(pl.multiple_of(b * 64 + s * 8, 8), 8)
            gated = base[at, :] + query[token_row(b, s), :] * (conv[at, :] + tree_sum(states))
            base[at, :] = gated
            conv[at, :] = gated * gated
        rows = [conv[token_row(b, s), :] for s in range(8)]
        squares[pl.ds(pl.multiple_of(b * 8, 8), 8), :] = tree_sum(rows)
        return tuple(states)

    def starts(pieces):
        return tuple(carry[p, i] * scale[p * PM + i] for p in pieces for i in range(PM))

    @pl.when(near_owner)
    def _():
        serve_behind()

    collect((2, 3))
    lax.fori_loop(0, BLOCKS, first_steps, starts((2, 3)))
    collect((0, 1))
    lax.fori_loop(0, BLOCKS, last_steps, starts((0, 1)))

    def exact_dot(a, b, dims):
        return lax.dot_general(a, b, (dims, ((), ())), preferred_element_type=F32)

    def split(a):
        high = a.astype(jnp.bfloat16)
        return high, (a - high.astype(F32)).astype(jnp.bfloat16)

    weight = jnp.full((8, LANES), 1.0 / (8 * C), jnp.bfloat16)
    high, low = split(squares[...])
    part[...] = exact_dot(weight, high, ((1,), (1,))) + exact_dot(weight, low, ((1,), (1,)))

    def y_copy(k):
        return pltpu.make_async_remote_copy(
            src_ref=part, dst_ref=parts.at[y],
            send_sem=y_send.at[k - 1], recv_sem=y_recv.at[y],
            device_id=device(x, z, core, lax.rem(y + k, NY)), device_id_type=MESH)

    @pl.when(y_rank < NY - 1)
    def _():
        pl.semaphore_wait(y_ready, NY - 1 - y_rank)

    for k in (4, 3, 5, 2, 6, 1, 7):
        y_copy(k).start()
    parts[y] = part[...]

    def relayout(b, _):
        rows = pl.ds(pl.multiple_of(b * 8, 8), 8)
        for j in range(LB):
            g_ref[rows, j * LANES:(j + 1) * LANES] = base[token_row(b, j), :] * gain_ref[j:j + 1, :]
        return 0

    lax.fori_loop(0, BLOCKS, relayout, 0)
    for p in range(PIECES):
        @pl.when(jnp.logical_not(is_me(p)))
        def _(p=p):
            fwd_copy(jnp.int32(p)).wait_send()

    @pl.when(is_owner)
    def _():
        for k in range(1, NX):
            @pl.when(x + k < NX)
            def _(k=k):
                x_copy(k).wait_send()
        for j in range(MEMBERS):
            @pl.when(me != j)
            def _(j=j):
                back_copy(j).wait_send()

            if j < NEAR:
                @pl.when(sends_far)
                def _(j=j):
                    far_copy(j).wait_send()

        @pl.when(first)
        def _():
            ex_copy(rows_with, 1, 0).wait_send()
            ex_copy(rows_with, 2, 1).wait_send()

        @pl.when(g == 1)
        def _():
            ex_copy(rows_with, 2, 0).wait_send()

        @pl.when(jnp.logical_and(g == 2, has_rows))
        def _():
            ex_copy(rows_before, 1, 1).wait_send()

    for k in range(1, NY):
        src = lax.rem(y + k, NY)
        pltpu.make_async_remote_copy(
            src_ref=part, dst_ref=parts.at[src],
            send_sem=y_send.at[0], recv_sem=y_recv.at[src],
            device_id=device(x, z, core, src), device_id_type=MESH).wait_recv()
    unit = jnp.ones((NY * 8, LANES), jnp.bfloat16)
    high, low = split(parts[...].reshape(NY * 8, LANES))
    power = exact_dot(high, unit, ((0,), (0,))) + exact_dot(low, unit, ((0,), (0,)))
    inv_ref[...] = lax.rsqrt(power + 1e-06)

    for k in range(1, NY):
        y_copy(k).wait_send()


def scale_rows(g_ref, inv_ref, o_hbm, rows_ref, sems):
    height = COUNT // SCALE_STEPS

    def out_copy(n):
        part = pl.ds(n * height, height)
        return pltpu.make_async_copy(rows_ref.at[part], o_hbm.at[part], sems.at[n])

    for n in range(SCALE_STEPS):
        for b in range(height // 16):
            rows = slice(n * height + b * 16, n * height + b * 16 + 16)
            norm = inv_ref[rows, :]
            for j in range(LB):
                cols = slice(j * LANES, (j + 1) * LANES)
                rows_ref[rows, cols] = (g_ref[rows, cols] * norm).astype(jnp.bfloat16)
        out_copy(n).start()
    for n in range(SCALE_STEPS):
        out_copy(n).wait()


def body(query, keys, values, rates, residues, skip, gain):
    in_vmem = lambda a: pltpu.with_memory_space_constraint(a, pltpu.VMEM)
    any_space = pl.BlockSpec(memory_space=pl.ANY)
    vmem = pltpu.VMEM
    dma = pltpu.SemaphoreType.DMA
    tile = (8, LANES)
    piece = (PM,) + tile
    gated, inv = pl.pallas_call(
        kernel,
        name="modal_scan",
        out_shape=(vmem((COUNT, WIDTH), F32), vmem((COUNT, LANES), F32)),
        in_specs=[any_space] * 7,
        out_specs=(pl.BlockSpec(memory_space=pltpu.VMEM), pl.BlockSpec(memory_space=pltpu.VMEM)),
        scratch_shapes=[
            vmem((COUNT, WIDTH), jnp.bfloat16),
            vmem((COUNT, WIDTH), jnp.bfloat16),
            vmem((COUNT, WIDTH), jnp.bfloat16),
            vmem((M, WIDTH), F32),
            vmem((M, WIDTH), F32),
            vmem(tile, F32),
            vmem(tile, F32),
            vmem((COUNT * 8, LANES), F32),
            vmem((256, LANES), F32),
            vmem((M,) + tile, F32),
            vmem((M,) + tile, F32),
            vmem((M,) + tile, F32),
            vmem((M,) + tile, F32),
            vmem((MEMBERS,) + piece, F32),
            vmem(piece, F32),
            vmem((NX,) + piece, F32),
            vmem(piece, F32),
            vmem(piece, F32),
            vmem((2,) + piece, F32),
            vmem((2, PIECES) + piece, F32),
            vmem((2, M) + tile, F32),
            vmem((4,) + piece, F32),
            vmem(piece, F32),
            vmem((MEMBERS,) + piece, F32),
            vmem((PIECES,) + piece, F32),
            vmem((COUNT * 8, LANES), F32),
            vmem((COUNT * 8, LANES), F32),
            vmem((COUNT * 8, LANES), F32),
            vmem((COUNT, LANES), F32),
            vmem(tile, F32),
            vmem((NY,) + tile, F32),
            dma((7,)),
            dma((PIECES,)), dma((MEMBERS,)),
            dma((NX - 1,)), dma((NX,)),
            dma((2,)), dma((2,)),
            dma((MEMBERS,)), dma((2, PIECES)),
            dma((MEMBERS,)), dma((PIECES,)),
            dma((NY - 1,)), dma((NY,)),
            pltpu.SemaphoreType.REGULAR, pltpu.SemaphoreType.REGULAR, pltpu.SemaphoreType.REGULAR,
        ],
        compiler_params=pltpu.CompilerParams(collective_id=0, has_side_effects=True),
    )(query, keys, values, rates, residues, skip.reshape(LB, LANES), gain.reshape(LB, LANES))
    return pl.pallas_call(
        scale_rows,
        name="scale_rows",
        out_shape=jax.ShapeDtypeStruct((COUNT, WIDTH), jnp.bfloat16),
        in_specs=[pl.BlockSpec(memory_space=pltpu.VMEM)] * 2,
        out_specs=pl.BlockSpec(memory_space=pl.ANY),
        scratch_shapes=[vmem((COUNT, WIDTH), jnp.bfloat16), dma((SCALE_STEPS,))],
    )(in_vmem(gated), in_vmem(inv))


def solution(mesh):
    in_specs = (
        P("ctx", "tp"), P("ctx", "tp"), P("ctx", "tp"),
        P(None, "tp"), P(None, "tp"), P("tp"), P("tp"),
    )
    return jax.shard_map(body, mesh=mesh, in_specs=in_specs, out_specs=P("ctx", "tp"), check_vma=False)
```

```python
import jax
import jax.numpy as jnp
from jax import lax
from jax.experimental import pallas as pl
from jax.experimental.pallas import tpu as pltpu
from jax.sharding import PartitionSpec as P

MESH = pl.DeviceIdType.MESH
F32 = jnp.float32

C = 8192
NX, NZ, NY = 4, 12, 8
LANES = 128
M = 16
COUNT = 128
WIDTH = 1024
LB = WIDTH // LANES
GROUP = 4
GROUPS = NZ // GROUP
MEMBERS = 2 * GROUP
PIECES = 4
PM = M // PIECES
BLOCKS = COUNT // 8
SEGS = 4
OWNER_BASE = (0, 0, 1)
NEAR = 4
SCALE_STEPS = 4
SEG_BLOCKS = BLOCKS // SEGS


def token_row(block, s):
    return pl.ds(block * 64 + s, 8, stride=8)


def kernel(q_hbm, k_hbm, v_hbm, rates_hbm, res_hbm, skip_hbm, gain_hbm, g_ref, inv_ref,
           q_ref, k_ref, v_ref, rates_ref, res_ref, skip_ref, gain_ref,
           driven, relay, dec, scale, leap, ends, fwd_buf, total, x_buf, rows_before, rows_with,
           ex_buf, far_buf, far_coef, coef,
           start_state, back_src, carry, query, conv, base, squares, part, parts,
           in_sem, fwd_send, fwd_recv, x_send, x_recv, ex_send, ex_recv, far_send, far_recv,
           back_send, back_recv, y_send, y_recv, x_ready, ex_ready, y_ready):
    ctx = lax.axis_index("ctx")
    y = lax.axis_index("tp")
    core = lax.rem(ctx, 2)
    chip = lax.div(ctx, 2)
    z = lax.rem(chip, NZ)
    x = lax.div(chip, NZ)
    g = lax.div(z, GROUP)
    r = lax.rem(z, GROUP)
    me = r * 2 + core
    first = g == 0
    owner_base = jnp.where(g == 2, OWNER_BASE[2], OWNER_BASE[0])
    is_owner = jnp.logical_and(r >= owner_base, r <= owner_base + 1)
    offset = jnp.where(r <= owner_base, 0, 1)
    pair = jnp.where(g == 1, 1 - offset, offset)
    y_rank = jnp.where(y < NY // 2, y, NY + NY // 2 - 1 - y)
    my_piece = pair * 2 + core
    has_rows = x >= 1

    def device(dx, dz, dc, dy):
        return ((dx * NZ + dz) * 2 + dc, dy)

    def owner_device(p):
        half = lax.div(p, 2)
        return device(x, g * GROUP + owner_base + jnp.where(g == 1, 1 - half, half), lax.rem(p, 2), y)

    def owner_in(group, p):
        half = lax.div(p, 2)
        return device(x, group * GROUP + OWNER_BASE[group] + (1 - half if group == 1 else half), lax.rem(p, 2), y)

    def peer_owner(group):
        return owner_in(group, my_piece)

    def is_me(p):
        return jnp.logical_and(is_owner, my_piece == p)

    def member_device(j):
        return device(x, g * GROUP + j // 2, j % 2, y)

    loads = []
    for n, (src, dst) in enumerate((
            (k_hbm, k_ref), (v_hbm, v_ref), (rates_hbm, rates_ref), (res_hbm, res_ref),
            (q_hbm, q_ref), (skip_hbm, skip_ref), (gain_hbm, gain_ref))):
        load = pltpu.make_async_copy(src, dst, in_sem.at[n])
        load.start()
        loads.append(load)

    barrier = pltpu.get_barrier_semaphore()

    def greet(dev):
        pl.semaphore_signal(barrier, inc=1, device_id=dev, device_id_type=MESH)

    def ready(sem, dev):
        pl.semaphore_signal(sem, inc=1, device_id=dev, device_id_type=MESH)

    def earlier_y(act):
        for k in range(1, NY):
            other = lax.rem(y + k, NY)
            rank = jnp.where(other < NY // 2, other, NY + NY // 2 - 1 - other)

            @pl.when(rank < y_rank)
            def _(other=other):
                act(device(x, z, core, other))

    for p in range(PIECES):
        @pl.when(jnp.logical_not(is_me(p)))
        def _(p=p):
            greet(owner_device(jnp.int32(p)))
    for k in range(1, NY):
        other = lax.rem(y + k, NY)
        rank = jnp.where(other < NY // 2, other, NY + NY // 2 - 1 - other)

        @pl.when(rank > y_rank)
        def _(other=other):
            greet(device(x, z, core, other))

    takes_far = jnp.logical_and(jnp.logical_and(first, r < NEAR // 2), has_rows)

    @pl.when(takes_far)
    def _():
        for group in range(1, GROUPS):
            for p in range(PIECES):
                greet(owner_in(group, jnp.int32(p)))

    @pl.when(is_owner)
    def _():
        for j in range(MEMBERS):
            @pl.when(jnp.logical_or(j // 2 < owner_base, j // 2 > owner_base + 1))
            def _(j=j):
                greet(member_device(j))
        for k in range(1, NX):
            @pl.when(x + k < NX)
            def _(k=k):
                greet(device(lax.rem(x + k, NX), z, core, y))

        @pl.when(first)
        def _():
            greet(peer_owner(1))

        @pl.when(g <= 1)
        def _():
            greet(peer_owner(2))

    expected = y_rank + jnp.where(
        is_owner,
        MEMBERS - 1 + x + g + jnp.where(jnp.logical_and(g >= 1, has_rows), NEAR, 0),
        PIECES)

    loads[2].wait()
    loads[3].wait()
    for which, (src, dst) in enumerate(((rates_ref, dec), (res_ref, scale))):
        for b in range(M // 8):
            for j in range(LB):
                relay[which * 128 + (b * 8 + j) * 8:which * 128 + (b * 8 + j) * 8 + 8, :] = (
                    src[b * 8:b * 8 + 8, j * LANES:(j + 1) * LANES])

    def mode_rate(m):
        return relay[token_row(m // 8, m % 8), :]

    for m in range(M):
        d = jnp.exp(-mode_rate(m))
        dec[m] = d
        leap[m] = jnp.exp(-mode_rate(m) * (COUNT // SEGS))
        scale[m] = relay[pl.ds(128 + (m // 8) * 64 + m % 8, 8, stride=8), :] * jnp.sqrt(1.0 - d * d)

    loads[0].wait()
    loads[1].wait()

    def make_driven(b, _):
        rows = pl.ds(pl.multiple_of(b * 16, 16), 16)
        for j in range(LB):
            cols = slice(j * LANES, (j + 1) * LANES)
            d = k_ref[rows, cols].astype(F32) * v_ref[rows, cols].astype(F32)
            driven[pl.ds(pl.multiple_of(b * 128 + j * 8, 8), 8), :] = d[:8]
            driven[pl.ds(pl.multiple_of(b * 128 + 64 + j * 8, 8), 8), :] = d[8:]
        return 0

    lax.fori_loop(0, COUNT // 16, make_driven, 0)

    def fwd_copy(p):
        return pltpu.make_async_remote_copy(
            src_ref=ends.at[pl.ds(p * PM, PM)], dst_ref=fwd_buf.at[me],
            send_sem=fwd_send.at[p], recv_sem=fwd_recv.at[me],
            device_id=owner_device(p), device_id_type=MESH)

    def answer_rows():
        @pl.when(is_owner)
        def _():
            for src in range(NX - 1):
                @pl.when(src < x)
                def _(src=src):
                    ready(x_ready, device(src, z, core, y))

    def answer():
        earlier_y(lambda dev: ready(y_ready, dev))

        @pl.when(jnp.logical_and(is_owner, g >= 1))
        def _():
            ready(ex_ready, peer_owner(0))

        @pl.when(jnp.logical_and(is_owner, g == 2))
        def _():
            ready(ex_ready, peer_owner(1))

    order = ((1 - pair) * 2, (1 - pair) * 2 + 1, pair * 2 + 1 - core, pair * 2 + core)
    for n_piece, p in enumerate(order):
        decays = [dec[p * PM + i] for i in range(PM)]

        def steps(b, states, decays=decays):
            states = list(states)
            for s in range(8):
                for seg in range(SEGS):
                    d = driven[token_row(seg * SEG_BLOCKS + b, s), :]
                    for i in range(PM):
                        n = seg * PM + i
                        states[n] = states[n] * decays[i] + d
            return tuple(states)

        zero = jnp.zeros((8, LANES), F32)
        states = lax.fori_loop(0, SEG_BLOCKS, steps, (zero,) * (SEGS * PM))
        for i in range(PM):
            m = p * PM + i
            s = states[i]
            for seg in range(1, SEGS):
                s = s * leap[m] + states[seg * PM + i]
            ends[m] = s
        if n_piece == 1:
            pl.semaphore_wait(barrier, expected)
        if n_piece >= 1:
            for ready_piece in order[0 if n_piece == 1 else n_piece:n_piece + 1]:
                @pl.when(jnp.logical_not(is_me(ready_piece)))
                def _(p=ready_piece):
                    fwd_copy(p).start()
        if n_piece == 1:
            answer_rows()
    answer()

    loads[4].wait()
    loads[5].wait()
    loads[6].wait()

    def make_query(b, _):
        rows = pl.ds(pl.multiple_of(b * 16, 16), 16)
        for j in range(LB):
            q = q_ref[rows, j * LANES:(j + 1) * LANES].astype(F32)
            query[pl.ds(pl.multiple_of(b * 128 + j * 8, 8), 8), :] = q[:8]
            query[pl.ds(pl.multiple_of(b * 128 + 64 + j * 8, 8), 8), :] = q[8:]
        return 0

    lax.fori_loop(0, COUNT // 16, make_query, 0)

    def tree_sum(terms):
        while len(terms) > 1:
            terms = [terms[i] + terms[i + 1] for i in range(0, len(terms), 2)]
        return terms[0]

    def conv_steps(b, states):
        states = list(states)
        for s in range(8):
            d = driven[token_row(b, s), :]
            terms = []
            for m in range(M):
                states[m] = states[m] * dec[m] + d
                terms.append(states[m] * scale[m])
            local = tree_sum(terms) + skip_ref[...] * d
            base[pl.ds(pl.multiple_of(b * 64 + s * 8, 8), 8), :] = query[token_row(b, s), :] * local
        return tuple(states)

    zero = jnp.zeros((8, LANES), F32)
    lax.fori_loop(0, BLOCKS, conv_steps, (zero,) * M)

    def back_copy(j):
        return pltpu.make_async_remote_copy(
            src_ref=back_src.at[j], dst_ref=carry.at[my_piece],
            send_sem=back_send.at[j], recv_sem=back_recv.at[my_piece],
            device_id=member_device(j), device_id_type=MESH)

    def x_copy(k):
        return pltpu.make_async_remote_copy(
            src_ref=total, dst_ref=x_buf.at[x],
            send_sem=x_send.at[k - 1], recv_sem=x_recv.at[x],
            device_id=device(lax.rem(x + k, NX), z, core, y), device_id_type=MESH)

    def ex_copy(src, group, slot):
        return pltpu.make_async_remote_copy(
            src_ref=src, dst_ref=ex_buf.at[slot],
            send_sem=ex_send.at[slot], recv_sem=ex_recv.at[slot],
            device_id=peer_owner(group), device_id_type=MESH)

    def far_copy(j):
        return pltpu.make_async_remote_copy(
            src_ref=rows_before, dst_ref=far_buf.at[g - 1, my_piece],
            send_sem=far_send.at[j], recv_sem=far_recv.at[g - 1, my_piece],
            device_id=device(x, j // 2, j % 2, y), device_id_type=MESH)

    def far_arrival(group, p):
        return pltpu.make_async_remote_copy(
            src_ref=rows_before, dst_ref=far_buf.at[group - 1, p],
            send_sem=far_send.at[0], recv_sem=far_recv.at[group - 1, p],
            device_id=owner_in(group, p),
            device_id_type=MESH)

    sends_far = jnp.logical_and(is_owner, jnp.logical_and(g >= 1, has_rows))
    span = COUNT * MEMBERS

    @pl.when(takes_far)
    def _():
        for m in range(M):
            rate = mode_rate(m)
            near = jnp.exp(-rate * (me * COUNT).astype(F32))
            far_coef[1, m] = near
            far_coef[0, m] = near * jnp.exp(-rate * span)

    @pl.when(is_owner)
    def _():
        for i in range(PM):
            m = my_piece * PM + i
            rate = relay[pl.ds(lax.div(m, 8) * 64 + lax.rem(m, 8), 8, stride=8), :]
            coef[0, i] = jnp.exp(-rate * COUNT)
            coef[1, i] = jnp.exp(-rate * span)
            coef[2, i] = jnp.exp(-rate * (2 * span))
            coef[3, i] = jnp.exp(-rate * (GROUPS * span))
            rows_before[i] = zero
            fwd_buf[me, i] = ends[m]
        for j in range(MEMBERS):
            @pl.when(me != j)
            def _(j=j):
                pltpu.make_async_remote_copy(
                    src_ref=ends.at[pl.ds(0, PM)], dst_ref=fwd_buf.at[j],
                    send_sem=fwd_send.at[0], recv_sem=fwd_recv.at[j],
                    device_id=member_device(j), device_id_type=MESH).wait_recv()
        for i in range(PM):
            s = fwd_buf[0, i]
            for j in range(1, MEMBERS):
                s = s * coef[0, i] + fwd_buf[j, i]
            total[i] = s
        @pl.when(x < NX - 1)
        def _():
            pl.semaphore_wait(x_ready, NX - 1 - x)

        for k in range(1, NX):
            @pl.when(x + k < NX)
            def _(k=k):
                x_copy(k).start()
        for src in range(NX - 1):
            @pl.when(src < x)
            def _(src=src):
                pltpu.make_async_remote_copy(
                    src_ref=total, dst_ref=x_buf.at[src],
                    send_sem=x_send.at[0], recv_sem=x_recv.at[src],
                    device_id=device(src, z, core, y), device_id_type=MESH).wait_recv()
                for i in range(PM):
                    rows_before[i] = rows_before[i] * coef[3, i] + x_buf[src, i]

        for j in range(NEAR):
            @pl.when(jnp.logical_and(sends_far, my_piece == j))
            def _(j=j):
                far_copy(j).start()

        for i in range(PM):
            rows_with[i] = rows_before[i] * coef[3, i] + total[i]
            start_state[i] = rows_before[i] * coef[2, i]

        @pl.when(g == 1)
        def _():
            pl.semaphore_wait(ex_ready, 1)
            ex_copy(rows_with, 2, 0).start()

        for j in range(NEAR):
            @pl.when(jnp.logical_and(sends_far, my_piece != j))
            def _(j=j):
                far_copy(j).start()

        @pl.when(jnp.logical_and(g == 2, has_rows))
        def _():
            ex_copy(rows_before, 1, 1).start()

        @pl.when(g == 1)
        def _():
            ex_copy(rows_with, 0, 0).wait_recv()
            for i in range(PM):
                start_state[i] = start_state[i] + ex_buf[0, i]

            @pl.when(has_rows)
            def _():
                ex_copy(rows_before, 2, 1).wait_recv()
                for i in range(PM):
                    start_state[i] = start_state[i] + ex_buf[1, i] * coef[1, i]

        @pl.when(g == 2)
        def _():
            for slot in range(2):
                ex_copy(rows_with, 1 - slot, slot).wait_recv()
            for i in range(PM):
                start_state[i] = start_state[i] + ex_buf[0, i] + ex_buf[1, i] * coef[1, i]

        def send_back(j):
            @pl.when(me != j)
            def _():
                back_copy(j).start()

            @pl.when(me == j)
            def _():
                for i in range(PM):
                    carry[my_piece, i] = back_src[j, i]

        for j in range(MEMBERS):
            for i in range(PM):
                if j == 0:
                    back_src[0, i] = start_state[i]
                else:
                    back_src[j, i] = back_src[j - 1, i] * coef[0, i] + fwd_buf[j - 1, i]
            if j < NEAR:
                send_back(j)
            else:
                @pl.when(jnp.logical_not(takes_far))
                def _(j=j):
                    send_back(j)

        @pl.when(first)
        def _():
            pl.semaphore_wait(ex_ready, 2)
            ex_copy(rows_with, 1, 0).start()
            ex_copy(rows_with, 2, 1).start()

    def serve_behind():
        for group in range(1, GROUPS):
            far_arrival(group, my_piece).wait_recv()
        for i in range(PM):
            far = far_buf[1, my_piece, i] + far_buf[0, my_piece, i] * coef[1, i]
            for _ in range(NEAR):
                far = far * coef[0, i]
            for j in range(NEAR, MEMBERS):
                back_src[j, i] = back_src[j, i] + far
                far = far * coef[0, i]
        for j in range(NEAR, MEMBERS):
            back_copy(j).start()

    def take(p):
        @pl.when(jnp.logical_not(is_me(p)))
        def _():
            pltpu.make_async_remote_copy(
                src_ref=back_src.at[0], dst_ref=carry.at[p],
                send_sem=back_send.at[0], recv_sem=back_recv.at[p],
                device_id=owner_device(jnp.int32(p)), device_id_type=MESH).wait_recv()

    def take_far(p):
        @pl.when(jnp.logical_not(is_me(p)))
        def _():
            for group in range(1, GROUPS):
                far_arrival(group, jnp.int32(p)).wait_recv()

    def add_far(p):
        for i in range(PM):
            m = p * PM + i
            carry[p, i] = carry[p, i] + far_buf[1, p, i] * far_coef[1, m] + far_buf[0, p, i] * far_coef[0, m]

    near_owner = jnp.logical_and(is_owner, takes_far)

    def collect(pieces):
        for p in pieces:
            take(p)

        @pl.when(takes_far)
        def _():
            for p in pieces:
                take_far(p)
            for p in pieces:
                add_far(p)

    def first_steps(b, states):
        states = list(states)
        for s in range(8):
            for n in range(M // 2):
                states[n] = states[n] * dec[M // 2 + n]
            conv[pl.ds(pl.multiple_of(b * 64 + s * 8, 8), 8), :] = tree_sum(states)
        return tuple(states)

    def last_steps(b, states):
        states = list(states)
        for s in range(8):
            for m in range(M // 2):
                states[m] = states[m] * dec[m]
            at = pl.ds(pl.multiple_of(b * 64 + s * 8, 8), 8)
            gated = base[at, :] + query[token_row(b, s), :] * (conv[at, :] + tree_sum(states))
            base[at, :] = gated
            conv[at, :] = gated * gated
        rows = [conv[token_row(b, s), :] for s in range(8)]
        squares[pl.ds(pl.multiple_of(b * 8, 8), 8), :] = tree_sum(rows)
        return tuple(states)

    def starts(pieces):
        return tuple(carry[p, i] * scale[p * PM + i] for p in pieces for i in range(PM))

    @pl.when(near_owner)
    def _():
        serve_behind()

    collect((2, 3))
    lax.fori_loop(0, BLOCKS, first_steps, starts((2, 3)))
    collect((0, 1))
    lax.fori_loop(0, BLOCKS, last_steps, starts((0, 1)))

    lane = lax.broadcasted_iota(jnp.int32, (8, LANES), 1)
    packed = zero
    for b in range(BLOCKS):
        row_sum = jnp.sum(squares[b * 8:b * 8 + 8, :], axis=1, keepdims=True)
        packed = jnp.where(lane == b, row_sum, packed)
    part[...] = packed * (1.0 / C)

    def y_copy(k):
        return pltpu.make_async_remote_copy(
            src_ref=part, dst_ref=parts.at[y],
            send_sem=y_send.at[k - 1], recv_sem=y_recv.at[y],
            device_id=device(x, z, core, lax.rem(y + k, NY)), device_id_type=MESH)

    @pl.when(y_rank < NY - 1)
    def _():
        pl.semaphore_wait(y_ready, NY - 1 - y_rank)

    for k in (4, 3, 5, 2, 6, 1, 7):
        y_copy(k).start()
    parts[y] = part[...]

    def relayout(b, _):
        rows = pl.ds(pl.multiple_of(b * 8, 8), 8)
        for j in range(LB):
            g_ref[rows, j * LANES:(j + 1) * LANES] = base[token_row(b, j), :] * gain_ref[j:j + 1, :]
        return 0

    lax.fori_loop(0, BLOCKS, relayout, 0)
    for p in range(PIECES):
        @pl.when(jnp.logical_not(is_me(p)))
        def _(p=p):
            fwd_copy(jnp.int32(p)).wait_send()

    @pl.when(is_owner)
    def _():
        for k in range(1, NX):
            @pl.when(x + k < NX)
            def _(k=k):
                x_copy(k).wait_send()
        for j in range(MEMBERS):
            @pl.when(me != j)
            def _(j=j):
                back_copy(j).wait_send()

            if j < NEAR:
                @pl.when(sends_far)
                def _(j=j):
                    far_copy(j).wait_send()

        @pl.when(first)
        def _():
            ex_copy(rows_with, 1, 0).wait_send()
            ex_copy(rows_with, 2, 1).wait_send()

        @pl.when(g == 1)
        def _():
            ex_copy(rows_with, 2, 0).wait_send()

        @pl.when(jnp.logical_and(g == 2, has_rows))
        def _():
            ex_copy(rows_before, 1, 1).wait_send()

    for k in range(1, NY):
        src = lax.rem(y + k, NY)
        pltpu.make_async_remote_copy(
            src_ref=part, dst_ref=parts.at[src],
            send_sem=y_send.at[0], recv_sem=y_recv.at[src],
            device_id=device(x, z, core, src), device_id_type=MESH).wait_recv()
    power = tree_sum([parts[n] for n in range(NY)])
    inv_ref[...] = lax.rsqrt(power + 1e-06)

    for k in range(1, NY):
        y_copy(k).wait_send()


def scale_rows(g_ref, inv_ref, o_hbm, rows_ref, sems):
    height = COUNT // SCALE_STEPS

    def out_copy(n):
        part = pl.ds(n * height, height)
        return pltpu.make_async_copy(rows_ref.at[part], o_hbm.at[part], sems.at[n])

    for n in range(SCALE_STEPS):
        for b in range(height // 16):
            rows = slice(n * height + b * 16, n * height + b * 16 + 16)
            block = rows.start // 8
            norm = jnp.concatenate(
                [jnp.broadcast_to(inv_ref[:, k:k + 1], (8, LANES)) for k in (block, block + 1)], axis=0)
            for j in range(LB):
                cols = slice(j * LANES, (j + 1) * LANES)
                rows_ref[rows, cols] = (g_ref[rows, cols] * norm).astype(jnp.bfloat16)
        out_copy(n).start()
    for n in range(SCALE_STEPS):
        out_copy(n).wait()


def body(query, keys, values, rates, residues, skip, gain):
    in_vmem = lambda a: pltpu.with_memory_space_constraint(a, pltpu.VMEM)
    any_space = pl.BlockSpec(memory_space=pl.ANY)
    vmem = pltpu.VMEM
    dma = pltpu.SemaphoreType.DMA
    tile = (8, LANES)
    piece = (PM,) + tile
    gated, inv = pl.pallas_call(
        kernel,
        name="modal_scan",
        out_shape=(vmem((COUNT, WIDTH), F32), vmem(tile, F32)),
        in_specs=[any_space] * 7,
        out_specs=(pl.BlockSpec(memory_space=pltpu.VMEM), pl.BlockSpec(memory_space=pltpu.VMEM)),
        scratch_shapes=[
            vmem((COUNT, WIDTH), jnp.bfloat16),
            vmem((COUNT, WIDTH), jnp.bfloat16),
            vmem((COUNT, WIDTH), jnp.bfloat16),
            vmem((M, WIDTH), F32),
            vmem((M, WIDTH), F32),
            vmem(tile, F32),
            vmem(tile, F32),
            vmem((COUNT * 8, LANES), F32),
            vmem((256, LANES), F32),
            vmem((M,) + tile, F32),
            vmem((M,) + tile, F32),
            vmem((M,) + tile, F32),
            vmem((M,) + tile, F32),
            vmem((MEMBERS,) + piece, F32),
            vmem(piece, F32),
            vmem((NX,) + piece, F32),
            vmem(piece, F32),
            vmem(piece, F32),
            vmem((2,) + piece, F32),
            vmem((2, PIECES) + piece, F32),
            vmem((2, M) + tile, F32),
            vmem((4,) + piece, F32),
            vmem(piece, F32),
            vmem((MEMBERS,) + piece, F32),
            vmem((PIECES,) + piece, F32),
            vmem((COUNT * 8, LANES), F32),
            vmem((COUNT * 8, LANES), F32),
            vmem((COUNT * 8, LANES), F32),
            vmem((COUNT, LANES), F32),
            vmem(tile, F32),
            vmem((NY,) + tile, F32),
            dma((7,)),
            dma((PIECES,)), dma((MEMBERS,)),
            dma((NX - 1,)), dma((NX,)),
            dma((2,)), dma((2,)),
            dma((MEMBERS,)), dma((2, PIECES)),
            dma((MEMBERS,)), dma((PIECES,)),
            dma((NY - 1,)), dma((NY,)),
            pltpu.SemaphoreType.REGULAR, pltpu.SemaphoreType.REGULAR, pltpu.SemaphoreType.REGULAR,
        ],
        compiler_params=pltpu.CompilerParams(collective_id=0, has_side_effects=True),
    )(query, keys, values, rates, residues, skip.reshape(LB, LANES), gain.reshape(LB, LANES))
    return pl.pallas_call(
        scale_rows,
        name="scale_rows",
        out_shape=jax.ShapeDtypeStruct((COUNT, WIDTH), jnp.bfloat16),
        in_specs=[pl.BlockSpec(memory_space=pltpu.VMEM)] * 2,
        out_specs=pl.BlockSpec(memory_space=pl.ANY),
        scratch_shapes=[vmem((COUNT, WIDTH), jnp.bfloat16), dma((SCALE_STEPS,))],
    )(in_vmem(gated), in_vmem(inv))


def solution(mesh):
    in_specs = (
        P("ctx", "tp"), P("ctx", "tp"), P("ctx", "tp"),
        P(None, "tp"), P(None, "tp"), P("tp"), P("tp"),
    )
    return jax.shard_map(body, mesh=mesh, in_specs=in_specs, out_specs=P("ctx", "tp"), check_vma=False)
```

```python
import jax
import jax.numpy as jnp
from jax import lax
from jax.experimental import pallas as pl
from jax.experimental.pallas import tpu as pltpu
from jax.sharding import PartitionSpec as P

MESH = pl.DeviceIdType.MESH
F32 = jnp.float32

C = 8192
NX, NZ, NY = 4, 12, 8
LANES = 128
M = 16
COUNT = 128
WIDTH = 1024
LB = WIDTH // LANES
GROUP = 4
GROUPS = NZ // GROUP
MEMBERS = 2 * GROUP
PIECES = 4
PM = M // PIECES
BLOCKS = COUNT // 8
SEGS = 4
OWNER_BASE = (0, 0, 1)
NEAR = 4
SCALE_STEPS = 4
SEG_BLOCKS = BLOCKS // SEGS


def token_row(block, s):
    return pl.ds(block * 64 + s, 8, stride=8)


def kernel(q_hbm, k_hbm, v_hbm, rates_hbm, res_hbm, skip_hbm, gain_hbm, g_ref, inv_ref,
           q_ref, k_ref, v_ref, rates_ref, res_ref, skip_ref, gain_ref,
           driven, relay, dec, scale, leap, ends, fwd_buf, total, x_buf, rows_before, rows_with,
           ex_buf, far_buf, far_coef, coef,
           start_state, back_src, carry, query, conv, base, squares, part, parts,
           in_sem, fwd_send, fwd_recv, x_send, x_recv, ex_send, ex_recv, far_send, far_recv,
           back_send, back_recv, y_send, y_recv, x_ready, ex_ready, y_ready, back_ready):
    ctx = lax.axis_index("ctx")
    y = lax.axis_index("tp")
    core = lax.rem(ctx, 2)
    chip = lax.div(ctx, 2)
    z = lax.rem(chip, NZ)
    x = lax.div(chip, NZ)
    g = lax.div(z, GROUP)
    r = lax.rem(z, GROUP)
    me = r * 2 + core
    first = g == 0
    owner_base = jnp.where(g == 2, OWNER_BASE[2], OWNER_BASE[0])
    is_owner = jnp.logical_and(r >= owner_base, r <= owner_base + 1)
    offset = jnp.where(r <= owner_base, 0, 1)
    pair = jnp.where(g == 1, 1 - offset, offset)
    y_rank = jnp.where(y < NY // 2, y, NY + NY // 2 - 1 - y)
    my_piece = pair * 2 + core
    has_rows = x >= 1

    def device(dx, dz, dc, dy):
        return ((dx * NZ + dz) * 2 + dc, dy)

    def owner_device(p):
        half = lax.div(p, 2)
        return device(x, g * GROUP + owner_base + jnp.where(g == 1, 1 - half, half), lax.rem(p, 2), y)

    def owner_in(group, p):
        half = lax.div(p, 2)
        return device(x, group * GROUP + OWNER_BASE[group] + (1 - half if group == 1 else half), lax.rem(p, 2), y)

    def peer_owner(group):
        return owner_in(group, my_piece)

    def is_me(p):
        return jnp.logical_and(is_owner, my_piece == p)

    def member_device(j):
        return device(x, g * GROUP + j // 2, j % 2, y)

    loads = []
    for n, (src, dst) in enumerate((
            (k_hbm, k_ref), (v_hbm, v_ref), (rates_hbm, rates_ref), (res_hbm, res_ref),
            (q_hbm, q_ref), (skip_hbm, skip_ref), (gain_hbm, gain_ref))):
        load = pltpu.make_async_copy(src, dst, in_sem.at[n])
        load.start()
        loads.append(load)

    barrier = pltpu.get_barrier_semaphore()

    def greet(dev):
        pl.semaphore_signal(barrier, inc=1, device_id=dev, device_id_type=MESH)

    def ready(sem, dev):
        pl.semaphore_signal(sem, inc=1, device_id=dev, device_id_type=MESH)

    def earlier_y(act):
        for k in range(1, NY):
            other = lax.rem(y + k, NY)
            rank = jnp.where(other < NY // 2, other, NY + NY // 2 - 1 - other)

            @pl.when(rank < y_rank)
            def _(other=other):
                act(device(x, z, core, other))

    is_late = r > owner_base + 1
    for p in range(PIECES):
        @pl.when(jnp.logical_not(jnp.logical_or(is_me(p), is_late)))
        def _(p=p):
            greet(owner_device(jnp.int32(p)))
    @pl.when(is_owner)
    def _():
        for j in range(MEMBERS):
            @pl.when(jnp.logical_or(j // 2 < owner_base, j // 2 > owner_base + 1))
            def _(j=j):
                greet(member_device(j))

    for k in range(1, NY):
        other = lax.rem(y + k, NY)
        rank = jnp.where(other < NY // 2, other, NY + NY // 2 - 1 - other)

        @pl.when(rank > y_rank)
        def _(other=other):
            greet(device(x, z, core, other))

    takes_far = jnp.logical_and(jnp.logical_and(first, r < NEAR // 2), has_rows)

    @pl.when(takes_far)
    def _():
        for group in range(1, GROUPS):
            for p in range(PIECES):
                greet(owner_in(group, jnp.int32(p)))

    @pl.when(is_owner)
    def _():
        for k in range(1, NX):
            @pl.when(x + k < NX)
            def _(k=k):
                greet(device(lax.rem(x + k, NX), z, core, y))

        @pl.when(first)
        def _():
            greet(peer_owner(1))

        @pl.when(g <= 1)
        def _():
            greet(peer_owner(2))

    expected = y_rank + jnp.where(
        is_owner,
        PIECES - 1 + 2 * owner_base + x + g + jnp.where(jnp.logical_and(g >= 1, has_rows), NEAR, 0),
        PIECES)

    loads[2].wait()
    loads[3].wait()
    for which, (src, dst) in enumerate(((rates_ref, dec), (res_ref, scale))):
        for b in range(M // 8):
            for j in range(LB):
                relay[which * 128 + (b * 8 + j) * 8:which * 128 + (b * 8 + j) * 8 + 8, :] = (
                    src[b * 8:b * 8 + 8, j * LANES:(j + 1) * LANES])

    def mode_rate(m):
        return relay[token_row(m // 8, m % 8), :]

    for m in range(M):
        d = jnp.exp(-mode_rate(m))
        dec[m] = d
        leap[m] = jnp.exp(-mode_rate(m) * (COUNT // SEGS))
        scale[m] = relay[pl.ds(128 + (m // 8) * 64 + m % 8, 8, stride=8), :] * jnp.sqrt(1.0 - d * d)

    loads[0].wait()
    loads[1].wait()

    def make_driven(b, _):
        rows = pl.ds(pl.multiple_of(b * 16, 16), 16)
        for j in range(LB):
            cols = slice(j * LANES, (j + 1) * LANES)
            d = k_ref[rows, cols].astype(F32) * v_ref[rows, cols].astype(F32)
            driven[pl.ds(pl.multiple_of(b * 128 + j * 8, 8), 8), :] = d[:8]
            driven[pl.ds(pl.multiple_of(b * 128 + 64 + j * 8, 8), 8), :] = d[8:]
        return 0

    lax.fori_loop(0, COUNT // 16, make_driven, 0)

    def fwd_copy(p):
        return pltpu.make_async_remote_copy(
            src_ref=ends.at[pl.ds(p * PM, PM)], dst_ref=fwd_buf.at[me],
            send_sem=fwd_send.at[p], recv_sem=fwd_recv.at[me],
            device_id=owner_device(p), device_id_type=MESH)

    def answer_rows():
        @pl.when(is_owner)
        def _():
            for src in range(NX - 1):
                @pl.when(src < x)
                def _(src=src):
                    ready(x_ready, device(src, z, core, y))

    def answer():
        for p in range(PIECES):
            @pl.when(is_late)
            def _(p=p):
                ready(back_ready, owner_device(jnp.int32(p)))

        earlier_y(lambda dev: ready(y_ready, dev))

        @pl.when(jnp.logical_and(is_owner, g >= 1))
        def _():
            ready(ex_ready, peer_owner(0))

        @pl.when(jnp.logical_and(is_owner, g == 2))
        def _():
            ready(ex_ready, peer_owner(1))

    order = ((1 - pair) * 2, (1 - pair) * 2 + 1, pair * 2 + 1 - core, pair * 2 + core)
    for n_piece, p in enumerate(order):
        decays = [dec[p * PM + i] for i in range(PM)]

        def steps(b, states, decays=decays):
            states = list(states)
            for s in range(8):
                for seg in range(SEGS):
                    d = driven[token_row(seg * SEG_BLOCKS + b, s), :]
                    for i in range(PM):
                        n = seg * PM + i
                        states[n] = states[n] * decays[i] + d
            return tuple(states)

        zero = jnp.zeros((8, LANES), F32)
        states = lax.fori_loop(0, SEG_BLOCKS, steps, (zero,) * (SEGS * PM))
        for i in range(PM):
            m = p * PM + i
            s = states[i]
            for seg in range(1, SEGS):
                s = s * leap[m] + states[seg * PM + i]
            ends[m] = s
        if n_piece == 0:
            pl.semaphore_wait(barrier, expected)
            answer_rows()
        if True:
            for ready_piece in (p,):
                @pl.when(jnp.logical_not(is_me(ready_piece)))
                def _(p=ready_piece):
                    fwd_copy(p).start()
    answer()

    loads[4].wait()
    loads[5].wait()
    loads[6].wait()

    def make_query(b, _):
        rows = pl.ds(pl.multiple_of(b * 16, 16), 16)
        for j in range(LB):
            q = q_ref[rows, j * LANES:(j + 1) * LANES].astype(F32)
            query[pl.ds(pl.multiple_of(b * 128 + j * 8, 8), 8), :] = q[:8]
            query[pl.ds(pl.multiple_of(b * 128 + 64 + j * 8, 8), 8), :] = q[8:]
        return 0

    lax.fori_loop(0, COUNT // 16, make_query, 0)

    def tree_sum(terms):
        while len(terms) > 1:
            terms = [terms[i] + terms[i + 1] for i in range(0, len(terms), 2)]
        return terms[0]

    def conv_steps(b, states):
        states = list(states)
        for s in range(8):
            d = driven[token_row(b, s), :]
            terms = []
            for m in range(M):
                states[m] = states[m] * dec[m] + d
                terms.append(states[m] * scale[m])
            local = tree_sum(terms) + skip_ref[...] * d
            base[pl.ds(pl.multiple_of(b * 64 + s * 8, 8), 8), :] = query[token_row(b, s), :] * local
        return tuple(states)

    zero = jnp.zeros((8, LANES), F32)
    lax.fori_loop(0, BLOCKS, conv_steps, (zero,) * M)

    def back_copy(j):
        return pltpu.make_async_remote_copy(
            src_ref=back_src.at[j], dst_ref=carry.at[my_piece],
            send_sem=back_send.at[j], recv_sem=back_recv.at[my_piece],
            device_id=member_device(j), device_id_type=MESH)

    def x_copy(k):
        return pltpu.make_async_remote_copy(
            src_ref=total, dst_ref=x_buf.at[x],
            send_sem=x_send.at[k - 1], recv_sem=x_recv.at[x],
            device_id=device(lax.rem(x + k, NX), z, core, y), device_id_type=MESH)

    def ex_copy(src, group, slot):
        return pltpu.make_async_remote_copy(
            src_ref=src, dst_ref=ex_buf.at[slot],
            send_sem=ex_send.at[slot], recv_sem=ex_recv.at[slot],
            device_id=peer_owner(group), device_id_type=MESH)

    def far_copy(j):
        return pltpu.make_async_remote_copy(
            src_ref=rows_before, dst_ref=far_buf.at[g - 1, my_piece],
            send_sem=far_send.at[j], recv_sem=far_recv.at[g - 1, my_piece],
            device_id=device(x, j // 2, j % 2, y), device_id_type=MESH)

    def far_arrival(group, p):
        return pltpu.make_async_remote_copy(
            src_ref=rows_before, dst_ref=far_buf.at[group - 1, p],
            send_sem=far_send.at[0], recv_sem=far_recv.at[group - 1, p],
            device_id=owner_in(group, p),
            device_id_type=MESH)

    sends_far = jnp.logical_and(is_owner, jnp.logical_and(g >= 1, has_rows))
    span = COUNT * MEMBERS

    @pl.when(takes_far)
    def _():
        for m in range(M):
            rate = mode_rate(m)
            near = jnp.exp(-rate * (me * COUNT).astype(F32))
            far_coef[1, m] = near
            far_coef[0, m] = near * jnp.exp(-rate * span)

    @pl.when(is_owner)
    def _():
        for i in range(PM):
            m = my_piece * PM + i
            rate = relay[pl.ds(lax.div(m, 8) * 64 + lax.rem(m, 8), 8, stride=8), :]
            coef[0, i] = jnp.exp(-rate * COUNT)
            coef[1, i] = jnp.exp(-rate * span)
            coef[2, i] = jnp.exp(-rate * (2 * span))
            coef[3, i] = jnp.exp(-rate * (GROUPS * span))
            rows_before[i] = zero
            fwd_buf[me, i] = ends[m]
        for j in range(MEMBERS):
            @pl.when(me != j)
            def _(j=j):
                pltpu.make_async_remote_copy(
                    src_ref=ends.at[pl.ds(0, PM)], dst_ref=fwd_buf.at[j],
                    send_sem=fwd_send.at[0], recv_sem=fwd_recv.at[j],
                    device_id=member_device(j), device_id_type=MESH).wait_recv()
        for i in range(PM):
            s = fwd_buf[0, i]
            for j in range(1, MEMBERS):
                s = s * coef[0, i] + fwd_buf[j, i]
            total[i] = s
        @pl.when(x < NX - 1)
        def _():
            pl.semaphore_wait(x_ready, NX - 1 - x)

        for k in range(1, NX):
            @pl.when(x + k < NX)
            def _(k=k):
                x_copy(k).start()
        for src in range(NX - 1):
            @pl.when(src < x)
            def _(src=src):
                pltpu.make_async_remote_copy(
                    src_ref=total, dst_ref=x_buf.at[src],
                    send_sem=x_send.at[0], recv_sem=x_recv.at[src],
                    device_id=device(src, z, core, y), device_id_type=MESH).wait_recv()
                for i in range(PM):
                    rows_before[i] = rows_before[i] * coef[3, i] + x_buf[src, i]

        for j in range(NEAR):
            @pl.when(jnp.logical_and(sends_far, my_piece == j))
            def _(j=j):
                far_copy(j).start()

        for i in range(PM):
            rows_with[i] = rows_before[i] * coef[3, i] + total[i]
            start_state[i] = rows_before[i] * coef[2, i]

        @pl.when(g == 1)
        def _():
            pl.semaphore_wait(ex_ready, 1)
            ex_copy(rows_with, 2, 0).start()

        for j in range(NEAR):
            @pl.when(jnp.logical_and(sends_far, my_piece != j))
            def _(j=j):
                far_copy(j).start()

        @pl.when(jnp.logical_and(g == 2, has_rows))
        def _():
            ex_copy(rows_before, 1, 1).start()

        @pl.when(g == 1)
        def _():
            ex_copy(rows_with, 0, 0).wait_recv()
            for i in range(PM):
                start_state[i] = start_state[i] + ex_buf[0, i]

            @pl.when(has_rows)
            def _():
                ex_copy(rows_before, 2, 1).wait_recv()
                for i in range(PM):
                    start_state[i] = start_state[i] + ex_buf[1, i] * coef[1, i]

        @pl.when(g == 2)
        def _():
            for slot in range(2):
                ex_copy(rows_with, 1 - slot, slot).wait_recv()
            for i in range(PM):
                start_state[i] = start_state[i] + ex_buf[0, i] + ex_buf[1, i] * coef[1, i]

        def send_back(j):
            @pl.when(me != j)
            def _():
                back_copy(j).start()

            @pl.when(me == j)
            def _():
                for i in range(PM):
                    carry[my_piece, i] = back_src[j, i]

        pl.semaphore_wait(back_ready, MEMBERS - PIECES - 2 * owner_base)
        for j in range(MEMBERS):
            for i in range(PM):
                if j == 0:
                    back_src[0, i] = start_state[i]
                else:
                    back_src[j, i] = back_src[j - 1, i] * coef[0, i] + fwd_buf[j - 1, i]
            if j < NEAR:
                send_back(j)
            else:
                @pl.when(jnp.logical_not(takes_far))
                def _(j=j):
                    send_back(j)

        @pl.when(first)
        def _():
            pl.semaphore_wait(ex_ready, 2)
            ex_copy(rows_with, 1, 0).start()
            ex_copy(rows_with, 2, 1).start()

    def serve_behind():
        for group in range(1, GROUPS):
            far_arrival(group, my_piece).wait_recv()
        for i in range(PM):
            far = far_buf[1, my_piece, i] + far_buf[0, my_piece, i] * coef[1, i]
            for _ in range(NEAR):
                far = far * coef[0, i]
            for j in range(NEAR, MEMBERS):
                back_src[j, i] = back_src[j, i] + far
                far = far * coef[0, i]
        for j in range(NEAR, MEMBERS):
            back_copy(j).start()

    def take(p):
        @pl.when(jnp.logical_not(is_me(p)))
        def _():
            pltpu.make_async_remote_copy(
                src_ref=back_src.at[0], dst_ref=carry.at[p],
                send_sem=back_send.at[0], recv_sem=back_recv.at[p],
                device_id=owner_device(jnp.int32(p)), device_id_type=MESH).wait_recv()

    def take_far(p):
        @pl.when(jnp.logical_not(is_me(p)))
        def _():
            for group in range(1, GROUPS):
                far_arrival(group, jnp.int32(p)).wait_recv()

    def add_far(p):
        for i in range(PM):
            m = p * PM + i
            carry[p, i] = carry[p, i] + far_buf[1, p, i] * far_coef[1, m] + far_buf[0, p, i] * far_coef[0, m]

    near_owner = jnp.logical_and(is_owner, takes_far)

    def collect(pieces):
        for p in pieces:
            take(p)

        @pl.when(takes_far)
        def _():
            for p in pieces:
                take_far(p)
            for p in pieces:
                add_far(p)

    def first_steps(b, states):
        states = list(states)
        for s in range(8):
            for n in range(M // 2):
                states[n] = states[n] * dec[M // 2 + n]
            conv[pl.ds(pl.multiple_of(b * 64 + s * 8, 8), 8), :] = tree_sum(states)
        return tuple(states)

    def last_steps(b, states):
        states = list(states)
        for s in range(8):
            for m in range(M // 2):
                states[m] = states[m] * dec[m]
            at = pl.ds(pl.multiple_of(b * 64 + s * 8, 8), 8)
            gated = base[at, :] + query[token_row(b, s), :] * (conv[at, :] + tree_sum(states))
            base[at, :] = gated
            conv[at, :] = gated * gated
        rows = [conv[token_row(b, s), :] for s in range(8)]
        squares[pl.ds(pl.multiple_of(b * 8, 8), 8), :] = tree_sum(rows)
        return tuple(states)

    def starts(pieces):
        return tuple(carry[p, i] * scale[p * PM + i] for p in pieces for i in range(PM))

    @pl.when(near_owner)
    def _():
        serve_behind()

    collect((2, 3))
    lax.fori_loop(0, BLOCKS, first_steps, starts((2, 3)))
    collect((0, 1))
    lax.fori_loop(0, BLOCKS, last_steps, starts((0, 1)))

    lane = lax.broadcasted_iota(jnp.int32, (8, LANES), 1)
    packed = zero
    for b in range(BLOCKS):
        row_sum = jnp.sum(squares[b * 8:b * 8 + 8, :], axis=1, keepdims=True)
        packed = jnp.where(lane == b, row_sum, packed)
    part[...] = packed * (1.0 / C)

    def y_copy(k):
        return pltpu.make_async_remote_copy(
            src_ref=part, dst_ref=parts.at[y],
            send_sem=y_send.at[k - 1], recv_sem=y_recv.at[y],
            device_id=device(x, z, core, lax.rem(y + k, NY)), device_id_type=MESH)

    @pl.when(y_rank < NY - 1)
    def _():
        pl.semaphore_wait(y_ready, NY - 1 - y_rank)

    for k in (4, 3, 5, 2, 6, 1, 7):
        y_copy(k).start()
    parts[y] = part[...]

    def relayout(b, _):
        rows = pl.ds(pl.multiple_of(b * 8, 8), 8)
        for j in range(LB):
            g_ref[rows, j * LANES:(j + 1) * LANES] = base[token_row(b, j), :] * gain_ref[j:j + 1, :]
        return 0

    lax.fori_loop(0, BLOCKS, relayout, 0)
    for p in range(PIECES):
        @pl.when(jnp.logical_not(is_me(p)))
        def _(p=p):
            fwd_copy(jnp.int32(p)).wait_send()

    @pl.when(is_owner)
    def _():
        for k in range(1, NX):
            @pl.when(x + k < NX)
            def _(k=k):
                x_copy(k).wait_send()
        for j in range(MEMBERS):
            @pl.when(me != j)
            def _(j=j):
                back_copy(j).wait_send()

            if j < NEAR:
                @pl.when(sends_far)
                def _(j=j):
                    far_copy(j).wait_send()

        @pl.when(first)
        def _():
            ex_copy(rows_with, 1, 0).wait_send()
            ex_copy(rows_with, 2, 1).wait_send()

        @pl.when(g == 1)
        def _():
            ex_copy(rows_with, 2, 0).wait_send()

        @pl.when(jnp.logical_and(g == 2, has_rows))
        def _():
            ex_copy(rows_before, 1, 1).wait_send()

    for k in range(1, NY):
        src = lax.rem(y + k, NY)
        pltpu.make_async_remote_copy(
            src_ref=part, dst_ref=parts.at[src],
            send_sem=y_send.at[0], recv_sem=y_recv.at[src],
            device_id=device(x, z, core, src), device_id_type=MESH).wait_recv()
    power = tree_sum([parts[n] for n in range(NY)])
    inv_ref[...] = lax.rsqrt(power + 1e-06)

    for k in range(1, NY):
        y_copy(k).wait_send()


def scale_rows(g_ref, inv_ref, o_hbm, rows_ref, sems):
    height = COUNT // SCALE_STEPS

    def out_copy(n):
        part = pl.ds(n * height, height)
        return pltpu.make_async_copy(rows_ref.at[part], o_hbm.at[part], sems.at[n])

    for n in range(SCALE_STEPS):
        for b in range(height // 16):
            rows = slice(n * height + b * 16, n * height + b * 16 + 16)
            block = rows.start // 8
            norm = jnp.concatenate(
                [jnp.broadcast_to(inv_ref[:, k:k + 1], (8, LANES)) for k in (block, block + 1)], axis=0)
            for j in range(LB):
                cols = slice(j * LANES, (j + 1) * LANES)
                rows_ref[rows, cols] = (g_ref[rows, cols] * norm).astype(jnp.bfloat16)
        out_copy(n).start()
    for n in range(SCALE_STEPS):
        out_copy(n).wait()


def body(query, keys, values, rates, residues, skip, gain):
    in_vmem = lambda a: pltpu.with_memory_space_constraint(a, pltpu.VMEM)
    any_space = pl.BlockSpec(memory_space=pl.ANY)
    vmem = pltpu.VMEM
    dma = pltpu.SemaphoreType.DMA
    tile = (8, LANES)
    piece = (PM,) + tile
    gated, inv = pl.pallas_call(
        kernel,
        name="modal_scan",
        out_shape=(vmem((COUNT, WIDTH), F32), vmem(tile, F32)),
        in_specs=[any_space] * 7,
        out_specs=(pl.BlockSpec(memory_space=pltpu.VMEM), pl.BlockSpec(memory_space=pltpu.VMEM)),
        scratch_shapes=[
            vmem((COUNT, WIDTH), jnp.bfloat16),
            vmem((COUNT, WIDTH), jnp.bfloat16),
            vmem((COUNT, WIDTH), jnp.bfloat16),
            vmem((M, WIDTH), F32),
            vmem((M, WIDTH), F32),
            vmem(tile, F32),
            vmem(tile, F32),
            vmem((COUNT * 8, LANES), F32),
            vmem((256, LANES), F32),
            vmem((M,) + tile, F32),
            vmem((M,) + tile, F32),
            vmem((M,) + tile, F32),
            vmem((M,) + tile, F32),
            vmem((MEMBERS,) + piece, F32),
            vmem(piece, F32),
            vmem((NX,) + piece, F32),
            vmem(piece, F32),
            vmem(piece, F32),
            vmem((2,) + piece, F32),
            vmem((2, PIECES) + piece, F32),
            vmem((2, M) + tile, F32),
            vmem((4,) + piece, F32),
            vmem(piece, F32),
            vmem((MEMBERS,) + piece, F32),
            vmem((PIECES,) + piece, F32),
            vmem((COUNT * 8, LANES), F32),
            vmem((COUNT * 8, LANES), F32),
            vmem((COUNT * 8, LANES), F32),
            vmem((COUNT, LANES), F32),
            vmem(tile, F32),
            vmem((NY,) + tile, F32),
            dma((7,)),
            dma((PIECES,)), dma((MEMBERS,)),
            dma((NX - 1,)), dma((NX,)),
            dma((2,)), dma((2,)),
            dma((MEMBERS,)), dma((2, PIECES)),
            dma((MEMBERS,)), dma((PIECES,)),
            dma((NY - 1,)), dma((NY,)),
            pltpu.SemaphoreType.REGULAR, pltpu.SemaphoreType.REGULAR,
            pltpu.SemaphoreType.REGULAR, pltpu.SemaphoreType.REGULAR,
        ],
        compiler_params=pltpu.CompilerParams(collective_id=0, has_side_effects=True),
    )(query, keys, values, rates, residues, skip.reshape(LB, LANES), gain.reshape(LB, LANES))
    return pl.pallas_call(
        scale_rows,
        name="scale_rows",
        out_shape=jax.ShapeDtypeStruct((COUNT, WIDTH), jnp.bfloat16),
        in_specs=[pl.BlockSpec(memory_space=pltpu.VMEM)] * 2,
        out_specs=pl.BlockSpec(memory_space=pl.ANY),
        scratch_shapes=[vmem((COUNT, WIDTH), jnp.bfloat16), dma((SCALE_STEPS,))],
    )(in_vmem(gated), in_vmem(inv))


def solution(mesh):
    in_specs = (
        P("ctx", "tp"), P("ctx", "tp"), P("ctx", "tp"),
        P(None, "tp"), P(None, "tp"), P("tp"), P("tp"),
    )
    return jax.shard_map(body, mesh=mesh, in_specs=in_specs, out_specs=P("ctx", "tp"), check_vma=False)
```

```python
import jax
import jax.numpy as jnp
from jax import lax
from jax.experimental import pallas as pl
from jax.experimental.pallas import tpu as pltpu
from jax.sharding import PartitionSpec as P

MESH = pl.DeviceIdType.MESH
F32 = jnp.float32

C = 8192
NX, NZ, NY = 4, 12, 8
LANES = 128
M = 16
COUNT = 128
WIDTH = 1024
LB = WIDTH // LANES
GROUP = 4
GROUPS = NZ // GROUP
MEMBERS = 2 * GROUP
PIECES = 4
PM = M // PIECES
BLOCKS = COUNT // 8
SEGS = 4
OWNER_BASE = (0, 0, 1)
NEAR = 4
SCALE_STEPS = 4
SEG_BLOCKS = BLOCKS // SEGS
SEG_LOG = (COUNT // SEGS).bit_length() - 1


def token_row(block, s):
    return pl.ds(block * 64 + s, 8, stride=8)


def kernel(q_hbm, k_hbm, v_hbm, rates_hbm, res_hbm, skip_hbm, gain_hbm, g_ref, inv_ref,
           q_ref, k_ref, v_ref, rates_ref, res_ref, skip_ref, gain_ref,
           driven, relay, dec, scale, ends, fwd_buf, total, x_buf, rows_before, rows_with,
           ex_buf, far_buf, far_coef, coef,
           start_state, back_src, carry, query, conv, base, squares, part, parts,
           in_sem, fwd_send, fwd_recv, x_send, x_recv, ex_send, ex_recv, far_send, far_recv,
           back_send, back_recv, y_send, y_recv, x_ready, ex_ready, y_ready, back_ready):
    ctx = lax.axis_index("ctx")
    y = lax.axis_index("tp")
    core = lax.rem(ctx, 2)
    chip = lax.div(ctx, 2)
    z = lax.rem(chip, NZ)
    x = lax.div(chip, NZ)
    g = lax.div(z, GROUP)
    r = lax.rem(z, GROUP)
    me = r * 2 + core
    first = g == 0
    owner_base = jnp.where(g == 2, OWNER_BASE[2], OWNER_BASE[0])
    is_owner = jnp.logical_and(r >= owner_base, r <= owner_base + 1)
    offset = jnp.where(r <= owner_base, 0, 1)
    pair = jnp.where(g == 1, 1 - offset, offset)
    y_rank = jnp.where(y < NY // 2, y, NY + NY // 2 - 1 - y)
    my_piece = pair * 2 + core
    has_rows = x >= 1

    def device(dx, dz, dc, dy):
        return ((dx * NZ + dz) * 2 + dc, dy)

    def owner_device(p):
        half = lax.div(p, 2)
        return device(x, g * GROUP + owner_base + jnp.where(g == 1, 1 - half, half), lax.rem(p, 2), y)

    def owner_in(group, p):
        half = lax.div(p, 2)
        return device(x, group * GROUP + OWNER_BASE[group] + (1 - half if group == 1 else half), lax.rem(p, 2), y)

    def peer_owner(group):
        return owner_in(group, my_piece)

    def is_me(p):
        return jnp.logical_and(is_owner, my_piece == p)

    def member_device(j):
        return device(x, g * GROUP + j // 2, j % 2, y)

    loads = []
    for n, (src, dst) in enumerate((
            (rates_hbm, rates_ref), (k_hbm, k_ref), (v_hbm, v_ref), (res_hbm, res_ref),
            (q_hbm, q_ref), (skip_hbm, skip_ref), (gain_hbm, gain_ref))):
        load = pltpu.make_async_copy(src, dst, in_sem.at[n])
        load.start()
        loads.append(load)

    barrier = pltpu.get_barrier_semaphore()

    def greet(dev):
        pl.semaphore_signal(barrier, inc=1, device_id=dev, device_id_type=MESH)

    def ready(sem, dev):
        pl.semaphore_signal(sem, inc=1, device_id=dev, device_id_type=MESH)

    def earlier_y(act):
        for k in range(1, NY):
            other = lax.rem(y + k, NY)
            rank = jnp.where(other < NY // 2, other, NY + NY // 2 - 1 - other)

            @pl.when(rank < y_rank)
            def _(other=other):
                act(device(x, z, core, other))

    is_late = r > owner_base + 1
    for p in range(PIECES):
        @pl.when(jnp.logical_not(jnp.logical_or(is_me(p), is_late)))
        def _(p=p):
            greet(owner_device(jnp.int32(p)))
    @pl.when(is_owner)
    def _():
        for j in range(MEMBERS):
            @pl.when(jnp.logical_or(j // 2 < owner_base, j // 2 > owner_base + 1))
            def _(j=j):
                greet(member_device(j))

    for k in range(1, NY):
        other = lax.rem(y + k, NY)
        rank = jnp.where(other < NY // 2, other, NY + NY // 2 - 1 - other)

        @pl.when(rank > y_rank)
        def _(other=other):
            greet(device(x, z, core, other))

    takes_far = jnp.logical_and(jnp.logical_and(first, r < NEAR // 2), has_rows)

    @pl.when(takes_far)
    def _():
        for group in range(1, GROUPS):
            for p in range(PIECES):
                greet(owner_in(group, jnp.int32(p)))

    @pl.when(is_owner)
    def _():
        for k in range(1, NX):
            @pl.when(x + k < NX)
            def _(k=k):
                greet(device(lax.rem(x + k, NX), z, core, y))

        @pl.when(first)
        def _():
            greet(peer_owner(1))

        @pl.when(g <= 1)
        def _():
            greet(peer_owner(2))

    expected = y_rank + jnp.where(
        is_owner,
        PIECES - 1 + 2 * owner_base + x + g + jnp.where(jnp.logical_and(g >= 1, has_rows), NEAR, 0),
        PIECES)

    def by_mode(src, top):
        for b in range(M // 8):
            for j in range(LB):
                at = top + (b * 8 + j) * 8
                relay[at:at + 8, :] = src[b * 8:b * 8 + 8, j * LANES:(j + 1) * LANES]

    def mode_rate(m):
        return relay[token_row(m // 8, m % 8), :]

    loads[0].wait()
    by_mode(rates_ref, 0)
    for m in range(M):
        dec[m] = jnp.exp(-mode_rate(m))

    loads[1].wait()
    loads[2].wait()

    def make_driven(b, _):
        rows = pl.ds(pl.multiple_of(b * 16, 16), 16)
        for j in range(LB):
            cols = slice(j * LANES, (j + 1) * LANES)
            d = k_ref[rows, cols].astype(F32) * v_ref[rows, cols].astype(F32)
            driven[pl.ds(pl.multiple_of(b * 128 + j * 8, 8), 8), :] = d[:8]
            driven[pl.ds(pl.multiple_of(b * 128 + 64 + j * 8, 8), 8), :] = d[8:]
        return 0

    lax.fori_loop(0, COUNT // 16, make_driven, 0)

    def fwd_copy(p):
        return pltpu.make_async_remote_copy(
            src_ref=ends.at[pl.ds(p * PM, PM)], dst_ref=fwd_buf.at[me],
            send_sem=fwd_send.at[p], recv_sem=fwd_recv.at[me],
            device_id=owner_device(p), device_id_type=MESH)

    def answer_rows():
        @pl.when(is_owner)
        def _():
            for src in range(NX - 1):
                @pl.when(src < x)
                def _(src=src):
                    ready(x_ready, device(src, z, core, y))

    def answer():
        for p in range(PIECES):
            @pl.when(is_late)
            def _(p=p):
                ready(back_ready, owner_device(jnp.int32(p)))

        earlier_y(lambda dev: ready(y_ready, dev))

        @pl.when(jnp.logical_and(is_owner, g >= 1))
        def _():
            ready(ex_ready, peer_owner(0))

        @pl.when(jnp.logical_and(is_owner, g == 2))
        def _():
            ready(ex_ready, peer_owner(1))

    order = ((1 - pair) * 2, (1 - pair) * 2 + 1, pair * 2 + 1 - core, pair * 2 + core)
    for n_piece, p in enumerate(order):
        decays = [dec[p * PM + i] for i in range(PM)]

        def steps(b, states, decays=decays):
            states = list(states)
            for s in range(8):
                for seg in range(SEGS):
                    d = driven[token_row(seg * SEG_BLOCKS + b, s), :]
                    for i in range(PM):
                        n = seg * PM + i
                        states[n] = states[n] * decays[i] + d
            return tuple(states)

        zero = jnp.zeros((8, LANES), F32)
        states = lax.fori_loop(0, SEG_BLOCKS, steps, (zero,) * (SEGS * PM))
        for i in range(PM):
            leap = decays[i]
            for _ in range(SEG_LOG):
                leap = leap * leap
            s = states[i]
            for seg in range(1, SEGS):
                s = s * leap + states[seg * PM + i]
            ends[p * PM + i] = s
        if n_piece == 0:
            pl.semaphore_wait(barrier, expected)
            answer_rows()
        if True:
            for ready_piece in (p,):
                @pl.when(jnp.logical_not(is_me(ready_piece)))
                def _(p=ready_piece):
                    fwd_copy(p).start()
    answer()

    loads[3].wait()
    by_mode(res_ref, 128)
    for m in range(M):
        d = dec[m]
        scale[m] = relay[pl.ds(128 + (m // 8) * 64 + m % 8, 8, stride=8), :] * jnp.sqrt(1.0 - d * d)

    loads[4].wait()
    loads[5].wait()
    loads[6].wait()

    def make_query(b, _):
        rows = pl.ds(pl.multiple_of(b * 16, 16), 16)
        for j in range(LB):
            q = q_ref[rows, j * LANES:(j + 1) * LANES].astype(F32)
            query[pl.ds(pl.multiple_of(b * 128 + j * 8, 8), 8), :] = q[:8]
            query[pl.ds(pl.multiple_of(b * 128 + 64 + j * 8, 8), 8), :] = q[8:]
        return 0

    lax.fori_loop(0, COUNT // 16, make_query, 0)

    def tree_sum(terms):
        while len(terms) > 1:
            terms = [terms[i] + terms[i + 1] for i in range(0, len(terms), 2)]
        return terms[0]

    def conv_steps(b, states):
        states = list(states)
        for s in range(8):
            d = driven[token_row(b, s), :]
            terms = []
            for m in range(M):
                states[m] = states[m] * dec[m] + d
                terms.append(states[m] * scale[m])
            local = tree_sum(terms) + skip_ref[...] * d
            base[pl.ds(pl.multiple_of(b * 64 + s * 8, 8), 8), :] = query[token_row(b, s), :] * local
        return tuple(states)

    zero = jnp.zeros((8, LANES), F32)
    lax.fori_loop(0, BLOCKS, conv_steps, (zero,) * M)

    def back_copy(j):
        return pltpu.make_async_remote_copy(
            src_ref=back_src.at[j], dst_ref=carry.at[my_piece],
            send_sem=back_send.at[j], recv_sem=back_recv.at[my_piece],
            device_id=member_device(j), device_id_type=MESH)

    def x_copy(k):
        return pltpu.make_async_remote_copy(
            src_ref=total, dst_ref=x_buf.at[x],
            send_sem=x_send.at[k - 1], recv_sem=x_recv.at[x],
            device_id=device(lax.rem(x + k, NX), z, core, y), device_id_type=MESH)

    def ex_copy(src, group, slot):
        return pltpu.make_async_remote_copy(
            src_ref=src, dst_ref=ex_buf.at[slot],
            send_sem=ex_send.at[slot], recv_sem=ex_recv.at[slot],
            device_id=peer_owner(group), device_id_type=MESH)

    def far_copy(j):
        return pltpu.make_async_remote_copy(
            src_ref=rows_before, dst_ref=far_buf.at[g - 1, my_piece],
            send_sem=far_send.at[j], recv_sem=far_recv.at[g - 1, my_piece],
            device_id=device(x, j // 2, j % 2, y), device_id_type=MESH)

    def far_arrival(group, p):
        return pltpu.make_async_remote_copy(
            src_ref=rows_before, dst_ref=far_buf.at[group - 1, p],
            send_sem=far_send.at[0], recv_sem=far_recv.at[group - 1, p],
            device_id=owner_in(group, p),
            device_id_type=MESH)

    sends_far = jnp.logical_and(is_owner, jnp.logical_and(g >= 1, has_rows))
    span = COUNT * MEMBERS

    @pl.when(takes_far)
    def _():
        for m in range(M):
            rate = mode_rate(m)
            near = jnp.exp(-rate * (me * COUNT).astype(F32))
            far_coef[1, m] = near
            far_coef[0, m] = near * jnp.exp(-rate * span)

    @pl.when(is_owner)
    def _():
        for i in range(PM):
            m = my_piece * PM + i
            rate = relay[pl.ds(lax.div(m, 8) * 64 + lax.rem(m, 8), 8, stride=8), :]
            coef[0, i] = jnp.exp(-rate * COUNT)
            coef[1, i] = jnp.exp(-rate * span)
            coef[2, i] = jnp.exp(-rate * (2 * span))
            coef[3, i] = jnp.exp(-rate * (GROUPS * span))
            rows_before[i] = zero
            fwd_buf[me, i] = ends[m]
        for j in range(MEMBERS):
            @pl.when(me != j)
            def _(j=j):
                pltpu.make_async_remote_copy(
                    src_ref=ends.at[pl.ds(0, PM)], dst_ref=fwd_buf.at[j],
                    send_sem=fwd_send.at[0], recv_sem=fwd_recv.at[j],
                    device_id=member_device(j), device_id_type=MESH).wait_recv()
        for i in range(PM):
            s = fwd_buf[0, i]
            for j in range(1, MEMBERS):
                s = s * coef[0, i] + fwd_buf[j, i]
            total[i] = s
        @pl.when(x < NX - 1)
        def _():
            pl.semaphore_wait(x_ready, NX - 1 - x)

        for k in range(1, NX):
            @pl.when(x + k < NX)
            def _(k=k):
                x_copy(k).start()
        for src in range(NX - 1):
            @pl.when(src < x)
            def _(src=src):
                pltpu.make_async_remote_copy(
                    src_ref=total, dst_ref=x_buf.at[src],
                    send_sem=x_send.at[0], recv_sem=x_recv.at[src],
                    device_id=device(src, z, core, y), device_id_type=MESH).wait_recv()
                for i in range(PM):
                    rows_before[i] = rows_before[i] * coef[3, i] + x_buf[src, i]

        for j in range(NEAR):
            @pl.when(jnp.logical_and(sends_far, my_piece == j))
            def _(j=j):
                far_copy(j).start()

        for i in range(PM):
            rows_with[i] = rows_before[i] * coef[3, i] + total[i]
            start_state[i] = rows_before[i] * coef[2, i]

        @pl.when(g == 1)
        def _():
            pl.semaphore_wait(ex_ready, 1)
            ex_copy(rows_with, 2, 0).start()

        for j in range(NEAR):
            @pl.when(jnp.logical_and(sends_far, my_piece != j))
            def _(j=j):
                far_copy(j).start()

        @pl.when(jnp.logical_and(g == 2, has_rows))
        def _():
            ex_copy(rows_before, 1, 1).start()

        @pl.when(g == 1)
        def _():
            ex_copy(rows_with, 0, 0).wait_recv()
            for i in range(PM):
                start_state[i] = start_state[i] + ex_buf[0, i]

            @pl.when(has_rows)
            def _():
                ex_copy(rows_before, 2, 1).wait_recv()
                for i in range(PM):
                    start_state[i] = start_state[i] + ex_buf[1, i] * coef[1, i]

        @pl.when(g == 2)
        def _():
            for slot in range(2):
                ex_copy(rows_with, 1 - slot, slot).wait_recv()
            for i in range(PM):
                start_state[i] = start_state[i] + ex_buf[0, i] + ex_buf[1, i] * coef[1, i]

        def send_back(j):
            @pl.when(me != j)
            def _():
                back_copy(j).start()

            @pl.when(me == j)
            def _():
                for i in range(PM):
                    carry[my_piece, i] = back_src[j, i]

        pl.semaphore_wait(back_ready, MEMBERS - PIECES - 2 * owner_base)
        for j in range(MEMBERS):
            for i in range(PM):
                if j == 0:
                    back_src[0, i] = start_state[i]
                else:
                    back_src[j, i] = back_src[j - 1, i] * coef[0, i] + fwd_buf[j - 1, i]
            if j < NEAR:
                send_back(j)
            else:
                @pl.when(jnp.logical_not(takes_far))
                def _(j=j):
                    send_back(j)

        @pl.when(first)
        def _():
            pl.semaphore_wait(ex_ready, 2)
            ex_copy(rows_with, 1, 0).start()
            ex_copy(rows_with, 2, 1).start()

    def serve_behind():
        for group in range(1, GROUPS):
            far_arrival(group, my_piece).wait_recv()
        for i in range(PM):
            far = far_buf[1, my_piece, i] + far_buf[0, my_piece, i] * coef[1, i]
            for _ in range(NEAR):
                far = far * coef[0, i]
            for j in range(NEAR, MEMBERS):
                back_src[j, i] = back_src[j, i] + far
                far = far * coef[0, i]
        for j in range(NEAR, MEMBERS):
            back_copy(j).start()

    def take(p):
        @pl.when(jnp.logical_not(is_me(p)))
        def _():
            pltpu.make_async_remote_copy(
                src_ref=back_src.at[0], dst_ref=carry.at[p],
                send_sem=back_send.at[0], recv_sem=back_recv.at[p],
                device_id=owner_device(jnp.int32(p)), device_id_type=MESH).wait_recv()

    def take_far(p):
        @pl.when(jnp.logical_not(is_me(p)))
        def _():
            for group in range(1, GROUPS):
                far_arrival(group, jnp.int32(p)).wait_recv()

    def add_far(p):
        for i in range(PM):
            m = p * PM + i
            carry[p, i] = carry[p, i] + far_buf[1, p, i] * far_coef[1, m] + far_buf[0, p, i] * far_coef[0, m]

    near_owner = jnp.logical_and(is_owner, takes_far)

    def collect(pieces):
        for p in pieces:
            take(p)

        @pl.when(takes_far)
        def _():
            for p in pieces:
                take_far(p)
            for p in pieces:
                add_far(p)

    def first_steps(b, states):
        states = list(states)
        for s in range(8):
            for n in range(M // 2):
                states[n] = states[n] * dec[M // 2 + n]
            conv[pl.ds(pl.multiple_of(b * 64 + s * 8, 8), 8), :] = tree_sum(states)
        return tuple(states)

    def last_steps(b, states):
        states = list(states)
        for s in range(8):
            for m in range(M // 2):
                states[m] = states[m] * dec[m]
            at = pl.ds(pl.multiple_of(b * 64 + s * 8, 8), 8)
            gated = base[at, :] + query[token_row(b, s), :] * (conv[at, :] + tree_sum(states))
            base[at, :] = gated
            conv[at, :] = gated * gated
        rows = [conv[token_row(b, s), :] for s in range(8)]
        squares[pl.ds(pl.multiple_of(b * 8, 8), 8), :] = tree_sum(rows)
        return tuple(states)

    def starts(pieces):
        return tuple(carry[p, i] * scale[p * PM + i] for p in pieces for i in range(PM))

    @pl.when(near_owner)
    def _():
        serve_behind()

    collect((2, 3))
    lax.fori_loop(0, BLOCKS, first_steps, starts((2, 3)))
    collect((0, 1))
    lax.fori_loop(0, BLOCKS, last_steps, starts((0, 1)))

    lane = lax.broadcasted_iota(jnp.int32, (8, LANES), 1)
    packed = zero
    for b in range(BLOCKS):
        row_sum = jnp.sum(squares[b * 8:b * 8 + 8, :], axis=1, keepdims=True)
        packed = jnp.where(lane == b, row_sum, packed)
    part[...] = packed * (1.0 / C)

    def y_copy(k):
        return pltpu.make_async_remote_copy(
            src_ref=part, dst_ref=parts.at[y],
            send_sem=y_send.at[k - 1], recv_sem=y_recv.at[y],
            device_id=device(x, z, core, lax.rem(y + k, NY)), device_id_type=MESH)

    @pl.when(y_rank < NY - 1)
    def _():
        pl.semaphore_wait(y_ready, NY - 1 - y_rank)

    for k in (4, 3, 5, 2, 6, 1, 7):
        y_copy(k).start()
    parts[y] = part[...]

    def relayout(b, _):
        rows = pl.ds(pl.multiple_of(b * 8, 8), 8)
        for j in range(LB):
            g_ref[rows, j * LANES:(j + 1) * LANES] = base[token_row(b, j), :] * gain_ref[j:j + 1, :]
        return 0

    lax.fori_loop(0, BLOCKS, relayout, 0)
    for p in range(PIECES):
        @pl.when(jnp.logical_not(is_me(p)))
        def _(p=p):
            fwd_copy(jnp.int32(p)).wait_send()

    @pl.when(is_owner)
    def _():
        for k in range(1, NX):
            @pl.when(x + k < NX)
            def _(k=k):
                x_copy(k).wait_send()
        for j in range(MEMBERS):
            @pl.when(me != j)
            def _(j=j):
                back_copy(j).wait_send()

            if j < NEAR:
                @pl.when(sends_far)
                def _(j=j):
                    far_copy(j).wait_send()

        @pl.when(first)
        def _():
            ex_copy(rows_with, 1, 0).wait_send()
            ex_copy(rows_with, 2, 1).wait_send()

        @pl.when(g == 1)
        def _():
            ex_copy(rows_with, 2, 0).wait_send()

        @pl.when(jnp.logical_and(g == 2, has_rows))
        def _():
            ex_copy(rows_before, 1, 1).wait_send()

    for k in range(1, NY):
        src = lax.rem(y + k, NY)
        pltpu.make_async_remote_copy(
            src_ref=part, dst_ref=parts.at[src],
            send_sem=y_send.at[0], recv_sem=y_recv.at[src],
            device_id=device(x, z, core, src), device_id_type=MESH).wait_recv()
    power = tree_sum([parts[n] for n in range(NY)])
    inv_ref[...] = lax.rsqrt(power + 1e-06)

    for k in range(1, NY):
        y_copy(k).wait_send()


def scale_rows(g_ref, inv_ref, o_hbm, rows_ref, sems):
    height = COUNT // SCALE_STEPS

    def out_copy(n):
        part = pl.ds(n * height, height)
        return pltpu.make_async_copy(rows_ref.at[part], o_hbm.at[part], sems.at[n])

    for n in range(SCALE_STEPS):
        for b in range(height // 16):
            rows = slice(n * height + b * 16, n * height + b * 16 + 16)
            block = rows.start // 8
            norm = jnp.concatenate(
                [jnp.broadcast_to(inv_ref[:, k:k + 1], (8, LANES)) for k in (block, block + 1)], axis=0)
            for j in range(LB):
                cols = slice(j * LANES, (j + 1) * LANES)
                rows_ref[rows, cols] = (g_ref[rows, cols] * norm).astype(jnp.bfloat16)
        out_copy(n).start()
    for n in range(SCALE_STEPS):
        out_copy(n).wait()


def body(query, keys, values, rates, residues, skip, gain):
    in_vmem = lambda a: pltpu.with_memory_space_constraint(a, pltpu.VMEM)
    any_space = pl.BlockSpec(memory_space=pl.ANY)
    vmem = pltpu.VMEM
    dma = pltpu.SemaphoreType.DMA
    tile = (8, LANES)
    piece = (PM,) + tile
    gated, inv = pl.pallas_call(
        kernel,
        name="modal_scan",
        out_shape=(vmem((COUNT, WIDTH), F32), vmem(tile, F32)),
        in_specs=[any_space] * 7,
        out_specs=(pl.BlockSpec(memory_space=pltpu.VMEM), pl.BlockSpec(memory_space=pltpu.VMEM)),
        scratch_shapes=[
            vmem((COUNT, WIDTH), jnp.bfloat16),
            vmem((COUNT, WIDTH), jnp.bfloat16),
            vmem((COUNT, WIDTH), jnp.bfloat16),
            vmem((M, WIDTH), F32),
            vmem((M, WIDTH), F32),
            vmem(tile, F32),
            vmem(tile, F32),
            vmem((COUNT * 8, LANES), F32),
            vmem((256, LANES), F32),
            vmem((M,) + tile, F32),
            vmem((M,) + tile, F32),
            vmem((M,) + tile, F32),
            vmem((MEMBERS,) + piece, F32),
            vmem(piece, F32),
            vmem((NX,) + piece, F32),
            vmem(piece, F32),
            vmem(piece, F32),
            vmem((2,) + piece, F32),
            vmem((2, PIECES) + piece, F32),
            vmem((2, M) + tile, F32),
            vmem((4,) + piece, F32),
            vmem(piece, F32),
            vmem((MEMBERS,) + piece, F32),
            vmem((PIECES,) + piece, F32),
            vmem((COUNT * 8, LANES), F32),
            vmem((COUNT * 8, LANES), F32),
            vmem((COUNT * 8, LANES), F32),
            vmem((COUNT, LANES), F32),
            vmem(tile, F32),
            vmem((NY,) + tile, F32),
            dma((7,)),
            dma((PIECES,)), dma((MEMBERS,)),
            dma((NX - 1,)), dma((NX,)),
            dma((2,)), dma((2,)),
            dma((MEMBERS,)), dma((2, PIECES)),
            dma((MEMBERS,)), dma((PIECES,)),
            dma((NY - 1,)), dma((NY,)),
            pltpu.SemaphoreType.REGULAR, pltpu.SemaphoreType.REGULAR,
            pltpu.SemaphoreType.REGULAR, pltpu.SemaphoreType.REGULAR,
        ],
        compiler_params=pltpu.CompilerParams(collective_id=0, has_side_effects=True),
    )(query, keys, values, rates, residues, skip.reshape(LB, LANES), gain.reshape(LB, LANES))
    return pl.pallas_call(
        scale_rows,
        name="scale_rows",
        out_shape=jax.ShapeDtypeStruct((COUNT, WIDTH), jnp.bfloat16),
        in_specs=[pl.BlockSpec(memory_space=pltpu.VMEM)] * 2,
        out_specs=pl.BlockSpec(memory_space=pl.ANY),
        scratch_shapes=[vmem((COUNT, WIDTH), jnp.bfloat16), dma((SCALE_STEPS,))],
    )(in_vmem(gated), in_vmem(inv))


def solution(mesh):
    in_specs = (
        P("ctx", "tp"), P("ctx", "tp"), P("ctx", "tp"),
        P(None, "tp"), P(None, "tp"), P("tp"), P("tp"),
    )
    return jax.shard_map(body, mesh=mesh, in_specs=in_specs, out_specs=P("ctx", "tp"), check_vma=False)
```
